256 devices in a mesh: row: 32 (over y, z), col: 8 (over x, core).
Axes of the slice: x: 4, y: 4, z: 8, core: 2. Of those that a mesh axis runs over, the one named last changes fastest.
Arguments:
- weights: bfloat16 [24576, 24576], P('row', 'col'), may hold values from -0.0390625 to 0.0390625
- rates: bfloat16 [5, 24576, 128], P(None, 'col'), may hold values from -0.94921875 to 0.94921875
Outputs:
- weight_grad: bfloat16 [24576, 24576], P('row', 'col')
The draws below stay inside these ranges and needn't reach their ends.
All inputs are finite; a program needn't handle non-finite values.
Results may differ from the reference program's by a relative error of at most 0.02.
Values may be sent and summed in bfloat16 or wider, within the bound.
No kernel may reach another device: no remote copies, remote signals or barrier semaphores. Data moves between devices by JAX's collectives and lax.ppermute only.
A program may use at most 128 MiB of HBM per device.

```python
import jax
import jax.numpy as jnp
from jax import lax

UNITS = 24576
TRIALS = 128
STEPS = 4


def block_scale(key, extent, shards, smallest, high):
    level, own = 1.0, jax.random.fold_in(key, 6)
    for axis_at, blocks in shards:
        draws = jnp.exp(jax.random.uniform(jax.random.fold_in(own, axis_at), (blocks,), jnp.float32, smallest / len(shards), high / len(shards)))
        level = level * jnp.repeat(draws, extent[axis_at] // blocks).reshape([-1 if axis == axis_at else 1 for axis in range(len(extent))])
    return level


def noise(stream_key, extent, spread, bound, pieces=(), held_as=jnp.bfloat16):
    loudness = block_scale(stream_key, extent, pieces, -0.22, 0.18) if pieces else 1.0
    entries = jax.random.normal(stream_key, extent, jnp.float32) * spread * loudness
    return jnp.minimum(jnp.maximum(entries, -bound), bound).astype(held_as)


def setup_inputs(seed: int = 0) -> dict:
    streams_of = jax.random.split(jax.random.key(seed), 3)
    weights = noise(streams_of[0], (UNITS, UNITS), UNITS ** -0.5, 0.0390625, ((0, 32), (1, 8)))
    rates = jnp.clip(jax.random.uniform(streams_of[1], (STEPS + 1, UNITS, TRIALS), jnp.float32, -0.94921875, 0.94921875) * block_scale(streams_of[1], (STEPS + 1, UNITS, TRIALS), ((1, 8),), -0.4, 0.0), -0.94921875, 0.94921875).astype(jnp.bfloat16)
    return dict(weights=weights, rates=rates)


def reference(weights, rates):
    ratef = rates.astype(jnp.float32)
    adjoint = ratef[STEPS] - ratef[0]
    grads = []
    for step in range(STEPS, 0, -1):
        local_grad = (adjoint * (1.0 - ratef[step] * ratef[step])).astype(jnp.bfloat16)
        grads.append(local_grad)
        if step > 1:
            adjoint = lax.dot_general(weights, local_grad, (((0,), (0,)), ((), ())), preferred_element_type=jnp.float32)
    stacked = jnp.concatenate(grads, axis=1)
    previous = jnp.concatenate([rates[step - 1] for step in range(STEPS, 0, -1)], axis=1)
    blocks = stacked.reshape(32, UNITS // 32, stacked.shape[1])

    def one_block(block):
        full = lax.dot_general(block, previous, (((1,), (1,)), ((), ())), preferred_element_type=jnp.float32)
        return full.astype(jnp.bfloat16)

    return lax.map(one_block, blocks).reshape(UNITS, UNITS)
```

```python
import jax
import jax.numpy as jnp
from jax import lax
from jax.experimental import pallas as pl
from jax.experimental.pallas import tpu as pltpu
from jax.sharding import Mesh, PartitionSpec as P

STEPS = 4
Y, Z, X, C = 4, 8, 4, 2
EVERY = ("y", "z", "x", "core")
SWAP = [(0, 1), (1, 0)]
HALF = 384
QUARTER = 768
TRIALS = 128


def flat(y, z, x, core):
    return ((y % Y * Z + z) * X + x % X) * C + core


def across(shift):
    return [
        (flat(y, z, x, core), flat(x, z, y + shift, core))
        for y in range(Y) for z in range(Z) for x in range(X) for core in range(C)
    ]


def from_root(shift):
    return [
        (flat(y, z, y, core), flat(y, z, y + shift, core))
        for y in range(Y) for z in range(Z) for core in range(C)
    ]


def back_kernel(core_ref, own_ref, oth_ref, w_ref, wp_ref, out_ref, g_ref):
    j = pl.program_id(0)
    core = core_ref[0]

    @pl.when(j == 0)
    def _():
        g_ref[:, pl.ds(pl.multiple_of(core * HALF, 128), HALF)] = own_ref[...]
        g_ref[:, pl.ds(pl.multiple_of((1 - core) * HALF, 128), HALF)] = oth_ref[...]

    def product(ref):
        out_ref[0] = jnp.dot(
            g_ref[...], ref[...], preferred_element_type=jnp.float32
        ).astype(jnp.bfloat16)

    @pl.when(j < 4)
    def _():
        product(w_ref)

    @pl.when(j >= 4)
    def _():
        product(wp_ref)


def back(core, own, oth, weights, partner):
    grid_spec = pltpu.PrefetchScalarGridSpec(
        num_scalar_prefetch=1,
        grid=(8,),
        in_specs=[
            pl.BlockSpec((TRIALS, HALF), lambda j, c: (0, 0)),
            pl.BlockSpec((TRIALS, HALF), lambda j, c: (0, 0)),
            pl.BlockSpec((QUARTER, HALF), lambda j, c: (0, 2 * jnp.minimum(j, 3) + c[0])),
            pl.BlockSpec((QUARTER, HALF), lambda j, c: (0, 2 * jnp.maximum(j - 4, 0) + c[0])),
        ],
        out_specs=pl.BlockSpec(
            (1, TRIALS, HALF),
            lambda j, c: (jnp.where(j < 4, c[0], 1 - c[0]) * 4 + j % 4, 0, 0),
        ),
        scratch_shapes=[pltpu.VMEM((TRIALS, QUARTER), jnp.bfloat16)],
    )
    return pl.pallas_call(
        back_kernel,
        grid_spec=grid_spec,
        out_shape=jax.ShapeDtypeStruct((8, TRIALS, HALF), jnp.bfloat16),
        cost_estimate=pl.CostEstimate(
            flops=2 * TRIALS * QUARTER * 3072, bytes_accessed=6_000_000, transcendentals=0
        ),
        name="back",
    )(core, own, oth, weights, partner)


TILE = 512


def outer_kernel(core_ref, *refs):
    owns, oths = refs[0:4], refs[4:8]
    rates_ref, out_ref, g_ref = refs[8], refs[9], refs[10]
    core = core_ref[0]

    @pl.when(pl.program_id(0) == 0)
    def _():
        for t in range(4):
            for ref, half in ((owns[t], core), (oths[t], 1 - core)):
                g_ref[pl.ds(pl.multiple_of(half * HALF, 16), HALF), t * TRIALS : (t + 1) * TRIALS] = (
                    ref[...].T
                )

    before = jnp.concatenate([rates_ref[t] for t in range(4)], axis=1)
    out_ref[...] = lax.dot_general(
        g_ref[...], before, (((1,), (1,)), ((), ())), preferred_element_type=jnp.float32
    ).astype(jnp.bfloat16)


def outer(core, owns, oths, rates):
    small = pl.BlockSpec((TRIALS, HALF), lambda j, c: (0, 0))
    grid_spec = pltpu.PrefetchScalarGridSpec(
        num_scalar_prefetch=1,
        grid=(3072 // TILE,),
        in_specs=[small] * 8 + [pl.BlockSpec((4, TILE, TRIALS), lambda j, c: (0, j, 0))],
        out_specs=pl.BlockSpec((QUARTER, TILE), lambda j, c: (0, j)),
        scratch_shapes=[pltpu.VMEM((QUARTER, 4 * TRIALS), jnp.bfloat16)],
    )
    return pl.pallas_call(
        outer_kernel,
        grid_spec=grid_spec,
        out_shape=jax.ShapeDtypeStruct((QUARTER, 3072), jnp.bfloat16),
        cost_estimate=pl.CostEstimate(
            flops=2 * 4 * TRIALS * QUARTER * 3072, bytes_accessed=10_000_000, transcendentals=0
        ),
        name="outer",
    )(core, *owns, *oths, rates)


def per_device(weights, rates):
    y, z, x, core = (lax.axis_index(a) for a in EVERY)
    partner = lax.ppermute(weights, "core", SWAP)
    quarter = lax.dynamic_slice_in_dim(rates, z % 4 * QUARTER, QUARTER, 1)
    turned = jnp.swapaxes(quarter, 1, 2)
    is_root_core = core == z // 4

    def at_row(block):
        axis = block.ndim - 1
        mine = lax.dynamic_slice_in_dim(block, core * HALF, HALF, axis)
        theirs = lax.dynamic_slice_in_dim(block, (1 - core) * HALF, HALF, axis)
        came = lax.ppermute(theirs, "core", SWAP)
        root = jnp.where(is_root_core, mine, came)
        parts = [lax.ppermute(root, EVERY, from_root(shift)) for shift in (1, 2, 3)]
        return jnp.where(x == y, root, parts[0] + parts[1] + parts[2])

    last = turned[STEPS].astype(jnp.float32)
    forcing = last - turned[0].astype(jnp.float32)
    own = at_row((forcing * (1.0 - last * last)).astype(jnp.bfloat16))
    oth = lax.ppermute(own, "core", SWAP)
    core_id = core.astype(jnp.int32).reshape(1)
    owns, oths = [own], [oth]
    row_rates = None
    for step in range(STEPS - 1, 0, -1):
        shares = back(core_id, own, oth, weights, partner)
        if row_rates is None:
            shares, later = lax.optimization_barrier((shares, turned[1:STEPS]))
            row_rates = at_row(later).astype(jnp.float32)
        parts = lax.all_to_all(shares, "z", 0, 0, tiled=True)
        summed = jnp.sum(parts.astype(jnp.float32), axis=0).astype(jnp.bfloat16)
        adjoint = sum(
            lax.ppermute(summed, EVERY, across(shift)).astype(jnp.float32) for shift in range(X)
        )
        rate = row_rates[step - 1]
        own = (adjoint * (1.0 - rate * rate)).astype(jnp.bfloat16)
        oth = lax.ppermute(own, "core", SWAP)
        owns.append(own)
        oths.append(oth)
    return outer(core_id, owns[::-1], oths[::-1], rates)


def solution(mesh):
    fine = Mesh(mesh.devices.reshape(Y, Z, X, C), EVERY)
    in_specs = (P(("y", "z"), ("x", "core")), P(None, ("x", "core"), None))
    out_specs = P(("y", "z"), ("x", "core"))
    return jax.shard_map(
        per_device, mesh=fine, in_specs=in_specs, out_specs=out_specs, check_vma=False
    )
```

```python
import jax
import jax.numpy as jnp
from jax import lax
from jax.experimental import pallas as pl
from jax.experimental.pallas import tpu as pltpu
from jax.sharding import Mesh, PartitionSpec as P

STEPS = 4
Y, Z, X, C = 4, 8, 4, 2
EVERY = ("y", "z", "x", "core")
SWAP = [(0, 1), (1, 0)]
HALF = 384
QUARTER = 768
TRIALS = 128
COLS = 3072
VMEM = pl.BlockSpec(memory_space=pltpu.VMEM)
SMEM = pl.BlockSpec(memory_space=pltpu.SMEM)
HBM = pl.BlockSpec(memory_space=pltpu.HBM)


def flat(y, z, x, core):
    return ((y % Y * Z + z) * X + x % X) * C + core


def across(shift):
    return [
        (flat(y, z, x, core), flat(x, z, y + shift, core))
        for y in range(Y) for z in range(Z) for x in range(X) for core in range(C)
    ]


def from_root(shift):
    return [
        (flat(y, z, y, core), flat(y, z, y + shift, core))
        for y in range(Y) for z in range(Z) for core in range(C)
    ]


def params(mib):
    return pltpu.CompilerParams(vmem_limit_bytes=mib << 20)


def cost(flops, moved):
    return pl.CostEstimate(flops=flops, bytes_accessed=moved, transcendentals=0)


def half(core):
    return pl.ds(pl.multiple_of(core * HALF, 128), HALF)


def first_kernel(at_ref, rates_ref, mine_ref, theirs_ref, last_ref, zero_ref, sems):
    core = at_ref[1]
    rows = pl.ds(pl.multiple_of(at_ref[0] * QUARTER, 16), QUARTER)
    copies = [
        pltpu.make_async_copy(rates_ref.at[STEPS, rows], last_ref, sems.at[0]),
        pltpu.make_async_copy(rates_ref.at[0, rows], zero_ref, sems.at[1]),
    ]
    for copy in copies:
        copy.start()
    for copy in copies:
        copy.wait()
    for out_ref, part in ((theirs_ref, 1 - core), (mine_ref, core)):
        part = pl.ds(pl.multiple_of(part * HALF, 16), HALF)
        last = last_ref[part, :].astype(jnp.float32)
        zero = zero_ref[part, :].astype(jnp.float32)
        out_ref[...] = ((last - zero) * (1.0 - last * last)).astype(jnp.bfloat16).T


def first(at, rates):
    shape = jax.ShapeDtypeStruct((TRIALS, HALF), jnp.bfloat16)
    return pl.pallas_call(
        first_kernel,
        in_specs=[SMEM, HBM],
        out_specs=[VMEM, VMEM],
        out_shape=[shape, shape],
        scratch_shapes=[
            pltpu.VMEM((QUARTER, TRIALS), jnp.bfloat16),
            pltpu.VMEM((QUARTER, TRIALS), jnp.bfloat16),
            pltpu.SemaphoreType.DMA((2,)),
        ],
        compiler_params=params(52),
        name="first",
    )(at, rates)


def split_kernel(at_ref, w_ref, theirs_ref, sems):
    columns = [pl.ds(pl.multiple_of((2 * q + 1 - at_ref[1]) * HALF, 128), HALF) for q in range(4)]
    copies = [
        pltpu.make_async_copy(w_ref.at[:, columns[q]], theirs_ref.at[q], sems.at[q])
        for q in range(4)
    ]
    for copy in copies:
        copy.start()
    for copy in copies:
        copy.wait()


def split(at, weights):
    return pl.pallas_call(
        split_kernel,
        in_specs=[SMEM, HBM],
        out_specs=VMEM,
        out_shape=jax.ShapeDtypeStruct((4, QUARTER, HALF), jnp.bfloat16),
        scratch_shapes=[pltpu.SemaphoreType.DMA((4,))],
        cost_estimate=cost(0, 4_718_592),
        compiler_params=params(50),
        name="split",
    )(at, weights)


def back_kernel(at_ref, own_ref, oth_ref, w_ref, theirs_ref, out_ref, g_ref, held_ref, sems):
    core = at_ref[1]
    copies = []
    for q in range(4):
        columns = pl.ds(pl.multiple_of((2 * q + core) * HALF, 128), HALF)
        copies.append(pltpu.make_async_copy(w_ref.at[:, columns], held_ref.at[q], sems.at[q]))
    for q in range(4):
        copies.append(pltpu.make_async_copy(theirs_ref.at[q], held_ref.at[4 + q], sems.at[4 + q]))
    for copy in copies:
        copy.start()
    g_ref[:, half(core)] = own_ref[...]
    g_ref[:, half(1 - core)] = oth_ref[...]
    for q in range(8):
        copies[q].wait()
        block = core if q < 4 else 1 - core
        out_ref[block * 4 + q % 4] = jnp.dot(
            g_ref[...], held_ref[q], preferred_element_type=jnp.float32
        ).astype(jnp.bfloat16)


def back(at, own, oth, weights, theirs):
    return pl.pallas_call(
        back_kernel,
        in_specs=[SMEM, VMEM, VMEM, HBM, HBM],
        out_specs=VMEM,
        out_shape=jax.ShapeDtypeStruct((8, TRIALS, HALF), jnp.bfloat16),
        scratch_shapes=[
            pltpu.VMEM((TRIALS, QUARTER), jnp.bfloat16),
            pltpu.VMEM((8, QUARTER, HALF), jnp.bfloat16),
            pltpu.SemaphoreType.DMA((8,)),
        ],
        cost_estimate=cost(2 * TRIALS * QUARTER * COLS, 6_000_000),
        compiler_params=params(48),
        name="back",
    )(at, own, oth, weights, theirs)


TILE = 1024


def gather_rows(core, pairs, g_ref):
    for t, (own_ref, oth_ref) in enumerate(pairs):
        for ref, part in ((own_ref, core), (oth_ref, 1 - core)):
            rows = pl.ds(pl.multiple_of(part * HALF, 16), HALF)
            g_ref[rows, t * TRIALS : (t + 1) * TRIALS] = ref[...].T


def early_kernel(at_ref, o3, o2, o1, p3, p2, p1, rates_ref, acc_ref, g_ref):
    j = pl.program_id(0)

    @pl.when(j == 0)
    def _():
        gather_rows(at_ref[1], ((o1, p1), (o2, p2), (o3, p3)), g_ref)

    before = jnp.concatenate([rates_ref[t] for t in range(1, STEPS)], axis=1)
    acc_ref[...] = lax.dot_general(
        g_ref[...], before, (((1,), (1,)), ((), ())), preferred_element_type=jnp.float32
    ).astype(jnp.bfloat16)


def early(at, owns, oths, rates):
    return pl.pallas_call(
        early_kernel,
        grid_spec=pltpu.PrefetchScalarGridSpec(
            num_scalar_prefetch=1,
            grid=(COLS // TILE,),
            in_specs=[VMEM] * 6 + [pl.BlockSpec((STEPS, TILE, TRIALS), lambda j, at: (0, j, 0))],
            out_specs=pl.BlockSpec((QUARTER, TILE), lambda j, at: (0, j)),
            scratch_shapes=[pltpu.VMEM((QUARTER, 3 * TRIALS), jnp.bfloat16)],
        ),
        out_shape=jax.ShapeDtypeStruct((QUARTER, COLS), jnp.bfloat16),
        cost_estimate=cost(2 * 3 * TRIALS * QUARTER * COLS, 10_000_000),
        compiler_params=params(50),
        name="early",
    )(at, *owns, *oths, rates)


def final_kernel(at_ref, own_ref, oth_ref, acc_ref, rates_ref, out_ref, g_ref):
    j = pl.program_id(0)

    @pl.when(j == 0)
    def _():
        gather_rows(at_ref[1], ((own_ref, oth_ref),), g_ref)

    out_ref[...] = (
        acc_ref[...].astype(jnp.float32)
        + lax.dot_general(
            g_ref[...], rates_ref[0], (((1,), (1,)), ((), ())), preferred_element_type=jnp.float32
        )
    ).astype(jnp.bfloat16)


def final(at, own, oth, acc, rates):
    return pl.pallas_call(
        final_kernel,
        grid_spec=pltpu.PrefetchScalarGridSpec(
            num_scalar_prefetch=1,
            grid=(COLS // TILE,),
            in_specs=[VMEM] * 2
            + [
                pl.BlockSpec((QUARTER, TILE), lambda j, at: (0, j)),
                pl.BlockSpec((1, TILE, TRIALS), lambda j, at: (0, j, 0)),
            ],
            out_specs=pl.BlockSpec((QUARTER, TILE), lambda j, at: (0, j)),
            scratch_shapes=[pltpu.VMEM((QUARTER, TRIALS), jnp.bfloat16)],
        ),
        out_shape=jax.ShapeDtypeStruct((QUARTER, COLS), jnp.bfloat16),
        cost_estimate=cost(2 * TRIALS * QUARTER * COLS, 11_000_000),
        compiler_params=params(52),
        name="final",
    )(at, own, oth, acc, rates)


def whole(weights, rates):
    y, z, x, core = (lax.axis_index(a) for a in EVERY)
    at = jnp.stack([z % 4, core]).astype(jnp.int32)
    is_root_core = core == z // 4

    def at_core(mine, theirs):
        return jnp.where(is_root_core, mine, lax.ppermute(theirs, "core", SWAP))

    def along_x(root):
        parts = [lax.ppermute(root, EVERY, from_root(shift)) for shift in (1, 2, 3)]
        return jnp.where(x == y, root, parts[0] + parts[1] + parts[2])

    root = at_core(*first(at, rates))
    own = along_x(root)
    theirs = split(at, lax.optimization_barrier((weights, root))[0])
    theirs = lax.ppermute(theirs, "core", SWAP)
    oth = lax.ppermute(own, "core", SWAP)
    owns, oths = [own], [oth]
    row_rates = None
    for step in range(STEPS - 1, 0, -1):
        shares = back(at, own, oth, weights, theirs)
        if row_rates is None:
            shares, later = lax.optimization_barrier((shares, rates[1:STEPS]))
            later = lax.dynamic_slice_in_dim(later, z % 4 * QUARTER, QUARTER, 1)
            halves = jnp.swapaxes(later.reshape(3, 2, HALF, TRIALS), 2, 3)
            halves = [
                lax.dynamic_index_in_dim(halves, part, 1, keepdims=False)
                for part in (core, 1 - core)
            ]
            row_rates = along_x(at_core(*halves))
        if step == 1:
            shares, owns, oths = lax.optimization_barrier((shares, owns, oths))
            acc = early(at, owns, oths, rates)
        parts = lax.all_to_all(shares, "z", 0, 0, tiled=True)
        summed = jnp.sum(parts.astype(jnp.float32), axis=0).astype(jnp.bfloat16)
        if step == 1:
            summed, acc = lax.optimization_barrier((summed, acc))
        adjoint = sum(
            lax.ppermute(summed, EVERY, across(shift)).astype(jnp.float32) for shift in range(X)
        )
        rate = row_rates[step - 1].astype(jnp.float32)
        own = (adjoint * (1.0 - rate * rate)).astype(jnp.bfloat16)
        oth = lax.ppermute(own, "core", SWAP)
        owns.append(own)
        oths.append(oth)
    return final(at, own, oth, acc, rates)


def solution(mesh):
    fine = Mesh(mesh.devices.reshape(Y, Z, X, C), EVERY)
    in_specs = (P(("y", "z"), ("x", "core")), P(None, ("x", "core"), None))
    out_specs = P(("y", "z"), ("x", "core"))
    return jax.shard_map(whole, mesh=fine, in_specs=in_specs, out_specs=out_specs, check_vma=False)
```

```python
import jax
import jax.numpy as jnp
from jax import lax
from jax.experimental import pallas as pl
from jax.experimental.pallas import tpu as pltpu
from jax.sharding import Mesh, PartitionSpec as P

STEPS = 4
Y, Z, X, C = 4, 8, 4, 2
EVERY = ("y", "z", "x", "core")
SWAP = [(0, 1), (1, 0)]
HALF = 384
QUARTER = 768
TRIALS = 128
SLICE = 32
SPLIT, ROWS, BACK, OUTER = 16, 16, 8, 52
COLS = 3072
VMEM = pl.BlockSpec(memory_space=pltpu.VMEM)
SMEM = pl.BlockSpec(memory_space=pltpu.SMEM)
HBM = pl.BlockSpec(memory_space=pltpu.HBM)


def flat(y, z, x, core):
    return ((y % Y * Z + z) * X + x % X) * C + core


def across(shift):
    return [
        (flat(y, z, x, core), flat(x, z, y + shift, core))
        for y in range(Y) for z in range(Z) for x in range(X) for core in range(C)
    ]


def from_root(shift):
    return [
        (flat(y, z, y, core), flat(y, z, y + shift, core))
        for y in range(Y) for z in range(Z) for core in range(C)
    ]


def params(mib):
    return pltpu.CompilerParams(vmem_limit_bytes=mib << 20)


def cost(flops, moved):
    return pl.CostEstimate(flops=flops, bytes_accessed=moved, transcendentals=0)


def half(core):
    return pl.ds(pl.multiple_of(core * HALF, 128), HALF)


def first_kernel(at_ref, rates_ref, mine_ref, theirs_ref, last_ref, zero_ref, sems):
    core = at_ref[1]
    rows = pl.ds(pl.multiple_of(at_ref[0] * QUARTER, 16), QUARTER)
    copies = [
        pltpu.make_async_copy(rates_ref.at[STEPS, rows], last_ref, sems.at[0]),
        pltpu.make_async_copy(rates_ref.at[0, rows], zero_ref, sems.at[1]),
    ]
    for copy in copies:
        copy.start()
    for copy in copies:
        copy.wait()
    for out_ref, part in ((theirs_ref, 1 - core), (mine_ref, core)):
        part = pl.ds(pl.multiple_of(part * HALF, 16), HALF)
        last = last_ref[part, :].astype(jnp.float32)
        zero = zero_ref[part, :].astype(jnp.float32)
        out_ref[...] = ((last - zero) * (1.0 - last * last)).astype(jnp.bfloat16).T


def first(at, rates):
    shape = jax.ShapeDtypeStruct((TRIALS, HALF), jnp.bfloat16)
    return pl.pallas_call(
        first_kernel,
        in_specs=[SMEM, HBM],
        out_specs=[VMEM, VMEM],
        out_shape=[shape, shape],
        scratch_shapes=[
            pltpu.VMEM((QUARTER, TRIALS), jnp.bfloat16),
            pltpu.VMEM((QUARTER, TRIALS), jnp.bfloat16),
            pltpu.SemaphoreType.DMA((2,)),
        ],
        compiler_params=params(52),
        name="first",
    )(at, rates)


def split_kernel(at_ref, w_ref, mine_ref, theirs_ref, sems):
    core = at_ref[1]
    copies = []
    for out_ref, part in ((theirs_ref, 1 - core), (mine_ref, core)):
        for q in range(4):
            columns = pl.ds(pl.multiple_of((2 * q + part) * HALF, 128), HALF)
            copies.append(
                pltpu.make_async_copy(w_ref.at[:, columns], out_ref.at[q], sems.at[len(copies)])
            )
    for copy in copies:
        copy.start()
    for copy in copies:
        copy.wait()


def split(at, weights):
    shape = jax.ShapeDtypeStruct((4, QUARTER, HALF), jnp.bfloat16)
    return pl.pallas_call(
        split_kernel,
        in_specs=[SMEM, HBM],
        out_specs=[VMEM, VMEM],
        out_shape=[shape, shape],
        scratch_shapes=[pltpu.SemaphoreType.DMA((8,))],
        cost_estimate=cost(0, 9_437_184),
        compiler_params=params(SPLIT),
        name="split",
    )(at, weights)


def rows_kernel(at_ref, rates_ref, mine_ref, theirs_ref, held_ref, turned_ref, sem):
    core = at_ref[1]
    rows = pl.ds(pl.multiple_of(at_ref[0] * QUARTER, 16), QUARTER)
    copy = pltpu.make_async_copy(rates_ref.at[1:STEPS, rows], held_ref, sem)
    copy.start()
    copy.wait()
    slot = pl.ds(pl.multiple_of(at_ref[2] * SLICE, SLICE), SLICE)
    for t in range(STEPS - 1):
        for out_ref, part in ((theirs_ref, 1 - core), (mine_ref, core)):
            turned_ref[...] = held_ref[t, pl.ds(pl.multiple_of(part * HALF, 16), HALF), :].T
            out_ref[t] = turned_ref[slot, :]


def rows(at, rates):
    shape = jax.ShapeDtypeStruct((STEPS - 1, SLICE, HALF), jnp.bfloat16)
    return pl.pallas_call(
        rows_kernel,
        in_specs=[SMEM, HBM],
        out_specs=[VMEM, VMEM],
        out_shape=[shape, shape],
        scratch_shapes=[
            pltpu.VMEM((STEPS - 1, QUARTER, TRIALS), jnp.bfloat16),
            pltpu.VMEM((TRIALS, HALF), jnp.bfloat16),
            pltpu.SemaphoreType.DMA,
        ],
        cost_estimate=cost(0, 600_000),
        compiler_params=params(ROWS),
        name="rows",
    )(at, rates)


def back_kernel(at_ref, own_ref, oth_ref, mine_ref, theirs_ref, out_ref, g_ref):
    core = at_ref[1]
    g_ref[:, half(core)] = own_ref[...]
    g_ref[:, half(1 - core)] = oth_ref[...]
    for ref, block in ((mine_ref, core), (theirs_ref, 1 - core)):
        for q in range(4):
            got = jnp.dot(g_ref[...], ref[q], preferred_element_type=jnp.float32)
            got = got.astype(jnp.bfloat16)
            for part in range(Y):
                out_ref[part, block * 4 + q] = got[part * SLICE : (part + 1) * SLICE]


def back(at, own, oth, mine, theirs):
    return pl.pallas_call(
        back_kernel,
        in_specs=[SMEM, VMEM, VMEM, VMEM, VMEM],
        out_specs=VMEM,
        out_shape=jax.ShapeDtypeStruct((Y, 8, SLICE, HALF), jnp.bfloat16),
        scratch_shapes=[pltpu.VMEM((TRIALS, QUARTER), jnp.bfloat16)],
        cost_estimate=cost(2 * TRIALS * QUARTER * COLS, 6_000_000),
        compiler_params=params(BACK),
        name="back",
    )(at, own, oth, mine, theirs)


TILE = 1024


def gather_rows(core, pairs, g_ref):
    for t, (own_ref, oth_ref) in enumerate(pairs):
        for ref, part in ((own_ref, core), (oth_ref, 1 - core)):
            rows = pl.ds(pl.multiple_of(part * HALF, 16), HALF)
            g_ref[rows, t * TRIALS : (t + 1) * TRIALS] = ref[...].T


def outer_kernel(at_ref, *refs):
    owns, oths, rates_ref, out_ref, g_ref = refs[:4], refs[4:8], *refs[8:]

    @pl.when(pl.program_id(0) == 0)
    def _():
        gather_rows(at_ref[1], tuple(zip(owns, oths)), g_ref)

    before = jnp.concatenate([rates_ref[t] for t in range(STEPS)], axis=1)
    out_ref[...] = lax.dot_general(
        g_ref[...], before, (((1,), (1,)), ((), ())), preferred_element_type=jnp.float32
    ).astype(jnp.bfloat16)


def outer(at, owns, oths, rates):
    return pl.pallas_call(
        outer_kernel,
        grid_spec=pltpu.PrefetchScalarGridSpec(
            num_scalar_prefetch=1,
            grid=(COLS // TILE,),
            in_specs=[VMEM] * 8 + [pl.BlockSpec((STEPS, TILE, TRIALS), lambda j, at: (0, j, 0))],
            out_specs=pl.BlockSpec((QUARTER, TILE), lambda j, at: (0, j)),
            scratch_shapes=[pltpu.VMEM((QUARTER, STEPS * TRIALS), jnp.bfloat16)],
        ),
        out_shape=jax.ShapeDtypeStruct((QUARTER, COLS), jnp.bfloat16),
        cost_estimate=cost(2 * STEPS * TRIALS * QUARTER * COLS, 8_000_000),
        compiler_params=params(OUTER),
        name="outer",
    )(at, *owns, *oths, rates)


def whole(weights, rates):
    y, z, x, core = (lax.axis_index(a) for a in EVERY)
    at = jnp.stack([z % 4, core, y]).astype(jnp.int32)

    def of_root_core(mine, theirs):
        return jnp.where(core == z // 4, mine, lax.ppermute(theirs, "core", SWAP))

    root = of_root_core(*first(at, rates))
    parts = [lax.ppermute(root, EVERY, from_root(shift)) for shift in (1, 2, 3)]
    own = jnp.where(x == y, root, parts[0] + parts[1] + parts[2])
    late_weights, late_rates, _ = lax.optimization_barrier((weights, rates, root))
    mine, theirs = split(at, late_weights)
    theirs = lax.ppermute(theirs, "core", SWAP)
    before = of_root_core(*rows(at, late_rates))
    oth = lax.ppermute(own, "core", SWAP)
    owns, oths = [own], [oth]
    for step in range(STEPS - 1, 0, -1):
        sums = back(at, own, oth, mine, theirs)
        for axis in ("y", "z"):
            sums = lax.all_to_all(sums, axis, 0, 0, tiled=True)
            sums = jnp.sum(sums.astype(jnp.float32), axis=0)
            if axis == "y":
                sums = sums.astype(jnp.bfloat16)
        rate = before[step - 1].astype(jnp.float32)
        share = (sums * (1.0 - rate * rate)).astype(jnp.bfloat16)
        slices = [lax.ppermute(share, EVERY, across(shift)) for shift in range(X)]
        turned = jnp.concatenate([slices[-s % X] for s in range(X)] * 2)
        own = lax.dynamic_slice_in_dim(turned, (X - x) % X * SLICE, TRIALS, 0)
        oth = lax.ppermute(own, "core", SWAP)
        owns.append(own)
        oths.append(oth)
    return outer(at, owns[::-1], oths[::-1], rates)


def solution(mesh):
    fine = Mesh(mesh.devices.reshape(Y, Z, X, C), EVERY)
    in_specs = (P(("y", "z"), ("x", "core")), P(None, ("x", "core"), None))
    out_specs = P(("y", "z"), ("x", "core"))
    return jax.shard_map(whole, mesh=fine, in_specs=in_specs, out_specs=out_specs, check_vma=False)
```

```python
import functools

import jax
import jax.numpy as jnp
from jax import lax
from jax.experimental import pallas as pl
from jax.experimental.pallas import tpu as pltpu
from jax.sharding import Mesh, PartitionSpec as P

STEPS = 4
Y, Z, X, C = 4, 8, 4, 2
EVERY = ("y", "z", "x", "core")
SWAP = [(0, 1), (1, 0)]
HALF = 384
QUARTER = 768
TRIALS = 128
SLICE = 32
SPLIT, ROWS, BACK, OUTER, KEEP = 52, 52, 8, 52, 48
COLS = 3072
VMEM = pl.BlockSpec(memory_space=pltpu.VMEM)
SMEM = pl.BlockSpec(memory_space=pltpu.SMEM)
HBM = pl.BlockSpec(memory_space=pltpu.HBM)


def flat(y, z, x, core):
    return ((y % Y * Z + z) * X + x % X) * C + core


def across(j):
    return [
        (flat(y, z, x, core), flat(x, z, y + j + 2 * core, core))
        for y in range(Y) for z in range(Z) for x in range(X) for core in range(C)
    ]


def from_root(shift):
    return [
        (flat(y, z, y, core), flat(y, z, y + shift, core))
        for y in range(Y) for z in range(Z) for core in range(C)
    ]


def params(mib):
    return pltpu.CompilerParams(vmem_limit_bytes=mib << 20)


def cost(flops, moved):
    return pl.CostEstimate(flops=flops, bytes_accessed=moved, transcendentals=0)


def half(core):
    return pl.ds(pl.multiple_of(core * HALF, 128), HALF)


def first_kernel(at_ref, rates_ref, mine_ref, theirs_ref, last_ref, zero_ref, sems):
    core = at_ref[1]
    rows = pl.ds(pl.multiple_of(at_ref[0] * QUARTER, 16), QUARTER)
    copies = [
        pltpu.make_async_copy(rates_ref.at[STEPS, rows], last_ref, sems.at[0]),
        pltpu.make_async_copy(rates_ref.at[0, rows], zero_ref, sems.at[1]),
    ]
    for copy in copies:
        copy.start()
    for copy in copies:
        copy.wait()
    for out_ref, part in ((theirs_ref, 1 - core), (mine_ref, core)):
        part = pl.ds(pl.multiple_of(part * HALF, 16), HALF)
        last = last_ref[part, :].astype(jnp.float32)
        zero = zero_ref[part, :].astype(jnp.float32)
        out_ref[...] = ((last - zero) * (1.0 - last * last)).astype(jnp.bfloat16).T


def first(at, rates):
    shape = jax.ShapeDtypeStruct((TRIALS, HALF), jnp.bfloat16)
    return pl.pallas_call(
        first_kernel,
        in_specs=[SMEM, HBM],
        out_specs=[VMEM, VMEM],
        out_shape=[shape, shape],
        scratch_shapes=[
            pltpu.VMEM((QUARTER, TRIALS), jnp.bfloat16),
            pltpu.VMEM((QUARTER, TRIALS), jnp.bfloat16),
            pltpu.SemaphoreType.DMA((2,)),
        ],
        compiler_params=params(52),
        name="first",
    )(at, rates)


def split_kernel(at_ref, w_ref, out_ref, sems, *, partner):
    part = 1 - at_ref[1] if partner else at_ref[1]
    copies = []
    for q in range(4):
        columns = pl.ds(pl.multiple_of((2 * q + part) * HALF, 128), HALF)
        copies.append(pltpu.make_async_copy(w_ref.at[:, columns], out_ref.at[q], sems.at[q]))
    for copy in copies:
        copy.start()
    for copy in copies:
        copy.wait()


def split(at, weights, partner):
    return pl.pallas_call(
        functools.partial(split_kernel, partner=partner),
        in_specs=[SMEM, HBM],
        out_specs=VMEM,
        out_shape=jax.ShapeDtypeStruct((4, QUARTER, HALF), jnp.bfloat16),
        scratch_shapes=[pltpu.SemaphoreType.DMA((4,))],
        cost_estimate=cost(0, 4_718_592),
        compiler_params=params(SPLIT if partner else KEEP),
        name="split",
    )(at, weights)


def rows_kernel(at_ref, rates_ref, mine_ref, theirs_ref, held_ref, turned_ref, sem):
    core = at_ref[1]
    rows = pl.ds(pl.multiple_of(at_ref[0] * QUARTER, 16), QUARTER)
    copy = pltpu.make_async_copy(rates_ref.at[1:STEPS, rows], held_ref, sem)
    copy.start()
    copy.wait()
    slot = pl.ds(pl.multiple_of(at_ref[2] * SLICE, SLICE), SLICE)
    for t in range(STEPS - 1):
        for out_ref, part in ((theirs_ref, 1 - core), (mine_ref, core)):
            turned_ref[...] = held_ref[t, pl.ds(pl.multiple_of(part * HALF, 16), HALF), :].T
            out_ref[t] = turned_ref[slot, :]


def rows(at, rates):
    shape = jax.ShapeDtypeStruct((STEPS - 1, SLICE, HALF), jnp.bfloat16)
    return pl.pallas_call(
        rows_kernel,
        in_specs=[SMEM, HBM],
        out_specs=[VMEM, VMEM],
        out_shape=[shape, shape],
        scratch_shapes=[
            pltpu.VMEM((STEPS - 1, QUARTER, TRIALS), jnp.bfloat16),
            pltpu.VMEM((TRIALS, HALF), jnp.bfloat16),
            pltpu.SemaphoreType.DMA,
        ],
        cost_estimate=cost(0, 600_000),
        compiler_params=params(ROWS),
        name="rows",
    )(at, rates)


def fill(at_ref, first_ref, second_ref, g_ref):
    core, x = at_ref[1], at_ref[3]
    for ref, part in ((first_ref, core), (second_ref, 1 - core)):
        if ref.shape == (TRIALS, HALF):
            g_ref[:, half(part)] = ref[...]
        else:
            for j in range(2):
                slot = (x + 2 * X - j - 2 * part) % X
                g_ref[pl.ds(pl.multiple_of(slot * SLICE, SLICE), SLICE), :] = ref[j]


def back_kernel(at_ref, first_ref, second_ref, mine_ref, theirs_ref, out_ref, g_ref, held_ref, sems):
    core = at_ref[1]
    copies = [
        pltpu.make_async_copy(theirs_ref.at[q], held_ref.at[q], sems.at[q]) for q in range(4)
    ]
    for copy in copies:
        copy.start()
    fill(at_ref, first_ref, second_ref, g_ref)
    for ref, block in ((mine_ref, core), (held_ref, 1 - core)):
        for q in range(4):
            if ref is held_ref:
                copies[q].wait()
            got = jnp.dot(g_ref[...], ref[q], preferred_element_type=jnp.float32)
            got = got.astype(jnp.bfloat16)
            for part in range(Y):
                out_ref[part, block * 4 + q] = got[part * SLICE : (part + 1) * SLICE]


def back(at, pair, mine, theirs):
    return pl.pallas_call(
        back_kernel,
        in_specs=[SMEM, VMEM, VMEM, VMEM, HBM],
        out_specs=[VMEM, VMEM],
        out_shape=[
            jax.ShapeDtypeStruct((Y, 8, SLICE, HALF), jnp.bfloat16),
            jax.ShapeDtypeStruct((TRIALS, QUARTER), jnp.bfloat16),
        ],
        scratch_shapes=[
            pltpu.VMEM((4, QUARTER, HALF), jnp.bfloat16),
            pltpu.SemaphoreType.DMA((4,)),
        ],
        cost_estimate=cost(2 * TRIALS * QUARTER * COLS, 6_000_000),
        compiler_params=params(BACK),
        name="back",
    )(at, *pair, mine, theirs)


TILE = 512
TILES = COLS // TILE


def outer_kernel(
    at_ref, g4, g3, g2, first_ref, second_ref, rates_ref, out_ref, g_ref, turned_ref, held_ref, done_ref, sems
):
    def came(j):
        columns = pl.ds(j * TILE, TILE)
        return pltpu.make_async_copy(rates_ref.at[0:STEPS, columns], held_ref.at[:, columns], sems.at[0, j])

    def went(j):
        columns = pl.ds(j * TILE, TILE)
        return pltpu.make_async_copy(done_ref.at[j], out_ref.at[:, columns], sems.at[1, j])

    for j in range(TILES):
        came(j).start()
    for t, ref in ((3, g4), (2, g3), (1, g2)):
        turned_ref[:, t * TRIALS : (t + 1) * TRIALS] = ref[...].T
    fill(at_ref, first_ref, second_ref, g_ref)
    turned_ref[:, :TRIALS] = g_ref[...].T
    for j in range(TILES):
        came(j).wait()
        columns = slice(j * TILE, (j + 1) * TILE)
        before = jnp.concatenate([held_ref[t, columns, :] for t in range(STEPS)], axis=1)
        done_ref[j] = lax.dot_general(
            turned_ref[...], before, (((1,), (1,)), ((), ())), preferred_element_type=jnp.float32
        ).astype(jnp.bfloat16)
        went(j).start()
    for j in range(TILES):
        went(j).wait()


def outer(at, full, pair, rates):
    return pl.pallas_call(
        outer_kernel,
        in_specs=[SMEM] + [VMEM] * 5 + [HBM],
        out_specs=HBM,
        out_shape=jax.ShapeDtypeStruct((QUARTER, COLS), jnp.bfloat16),
        scratch_shapes=[
            pltpu.VMEM((TRIALS, QUARTER), jnp.bfloat16),
            pltpu.VMEM((QUARTER, STEPS * TRIALS), jnp.bfloat16),
            pltpu.VMEM((STEPS, COLS, TRIALS), jnp.bfloat16),
            pltpu.VMEM((TILES, QUARTER, TILE), jnp.bfloat16),
            pltpu.SemaphoreType.DMA((2, TILES)),
        ],
        cost_estimate=cost(2 * STEPS * TRIALS * QUARTER * COLS, 8_000_000),
        compiler_params=params(OUTER),
        name="outer",
    )(at, *full, *pair, rates)


def whole(weights, rates):
    y, z, x, core = (lax.axis_index(a) for a in EVERY)
    at = jnp.stack([z % 4, core, y, x]).astype(jnp.int32)

    def swapped(array):
        return lax.ppermute(array, "core", SWAP)

    def of_root_core(mine, theirs):
        return jnp.where(core == z // 4, mine, swapped(theirs))

    root = of_root_core(*first(at, rates))
    parts = [lax.ppermute(root, EVERY, from_root(shift)) for shift in (1, 2, 3)]
    own = jnp.where(x == y, root, parts[0] + parts[1] + parts[2])
    late_weights, late_rates, _ = lax.optimization_barrier((weights, rates, root))
    theirs = swapped(split(at, late_weights, True))
    mine = split(at, late_weights, False)
    before = of_root_core(*rows(at, late_rates))
    pair = (own, swapped(own))
    full = []
    for step in range(STEPS - 1, 0, -1):
        sums, whole_grad = back(at, pair, mine, theirs)
        full.append(whole_grad)
        for axis in ("y", "z"):
            sums = lax.all_to_all(sums, axis, 0, 0, tiled=True)
            sums = jnp.sum(sums.astype(jnp.float32), axis=0)
            if axis == "y":
                sums = sums.astype(jnp.bfloat16)
        rate = before[step - 1].astype(jnp.float32)
        share = (sums * (1.0 - rate * rate)).astype(jnp.bfloat16)
        other = swapped(share)
        share = jnp.where(
            core == 0, jnp.concatenate([share, other], 1), jnp.concatenate([other, share], 1)
        )
        slices = jnp.stack([lax.ppermute(share, EVERY, across(j)) for j in range(2)])
        pair = (slices, swapped(slices))
    return outer(at, full, pair, rates)


def solution(mesh):
    fine = Mesh(mesh.devices.reshape(Y, Z, X, C), EVERY)
    in_specs = (P(("y", "z"), ("x", "core")), P(None, ("x", "core"), None))
    out_specs = P(("y", "z"), ("x", "core"))
    return jax.shard_map(whole, mesh=fine, in_specs=in_specs, out_specs=out_specs, check_vma=False)
```

```python
import functools

import jax
import jax.numpy as jnp
from jax import lax
from jax.experimental import pallas as pl
from jax.experimental.pallas import tpu as pltpu
from jax.sharding import Mesh, PartitionSpec as P

STEPS = 4
Y, Z, X, C = 4, 8, 4, 2
EVERY = ("y", "z", "x", "core")
SWAP = [(0, 1), (1, 0)]
HALF = 384
QUARTER = 768
TRIALS = 128
SLICE = 32
SPLIT, ROWS, BACK, OUTER, KEEP = 48, 52, 8, 52, 48
COLS = 3072
VMEM = pl.BlockSpec(memory_space=pltpu.VMEM)
SMEM = pl.BlockSpec(memory_space=pltpu.SMEM)
HBM = pl.BlockSpec(memory_space=pltpu.HBM)


def flat(y, z, x, core):
    return ((y % Y * Z + z) * X + x % X) * C + core


def across(j):
    return [
        (flat(y, z, x, core), flat(x, z, y + j + 2 * core, core))
        for y in range(Y) for z in range(Z) for x in range(X) for core in range(C)
    ]


def from_root(shift):
    return [
        (flat(y, z, y, core), flat(y, z, y + shift, core))
        for y in range(Y) for z in range(Z) for core in range(C)
    ]


def params(mib):
    return pltpu.CompilerParams(vmem_limit_bytes=mib << 20)


def cost(flops, moved):
    return pl.CostEstimate(flops=flops, bytes_accessed=moved, transcendentals=0)


def half(core):
    return pl.ds(pl.multiple_of(core * HALF, 128), HALF)


def first_kernel(at_ref, rates_ref, mine_ref, theirs_ref, last_ref, zero_ref, sems):
    core = at_ref[1]
    rows = pl.ds(pl.multiple_of(at_ref[0] * QUARTER, 16), QUARTER)
    copies = [
        pltpu.make_async_copy(rates_ref.at[STEPS, rows], last_ref, sems.at[0]),
        pltpu.make_async_copy(rates_ref.at[0, rows], zero_ref, sems.at[1]),
    ]
    for copy in copies:
        copy.start()
    for copy in copies:
        copy.wait()
    for out_ref, part in ((theirs_ref, 1 - core), (mine_ref, core)):
        part = pl.ds(pl.multiple_of(part * HALF, 16), HALF)
        last = last_ref[part, :].astype(jnp.float32)
        zero = zero_ref[part, :].astype(jnp.float32)
        out_ref[...] = ((last - zero) * (1.0 - last * last)).astype(jnp.bfloat16).T


def first(at, rates):
    shape = jax.ShapeDtypeStruct((TRIALS, HALF), jnp.bfloat16)
    return pl.pallas_call(
        first_kernel,
        in_specs=[SMEM, HBM],
        out_specs=[VMEM, VMEM],
        out_shape=[shape, shape],
        scratch_shapes=[
            pltpu.VMEM((QUARTER, TRIALS), jnp.bfloat16),
            pltpu.VMEM((QUARTER, TRIALS), jnp.bfloat16),
            pltpu.SemaphoreType.DMA((2,)),
        ],
        compiler_params=params(52),
        name="first",
    )(at, rates)


def split_kernel(at_ref, w_ref, out_ref, sems, *, partner):
    part = 1 - at_ref[1] if partner else at_ref[1]
    copies = []
    for q in range(4):
        columns = pl.ds(pl.multiple_of((2 * q + part) * HALF, 128), HALF)
        copies.append(pltpu.make_async_copy(w_ref.at[:, columns], out_ref.at[q], sems.at[q]))
    for copy in copies:
        copy.start()
    for copy in copies:
        copy.wait()


def split(at, weights, partner):
    return pl.pallas_call(
        functools.partial(split_kernel, partner=partner),
        in_specs=[SMEM, HBM],
        out_specs=VMEM,
        out_shape=jax.ShapeDtypeStruct((4, QUARTER, HALF), jnp.bfloat16),
        scratch_shapes=[pltpu.SemaphoreType.DMA((4,))],
        cost_estimate=cost(0, 4_718_592),
        compiler_params=params(SPLIT if partner else KEEP),
        name="split",
    )(at, weights)


def rows_kernel(at_ref, rates_ref, mine_ref, theirs_ref, held_ref, turned_ref, sem):
    core = at_ref[1]
    rows = pl.ds(pl.multiple_of(at_ref[0] * QUARTER, 16), QUARTER)
    copy = pltpu.make_async_copy(rates_ref.at[1:STEPS, rows], held_ref, sem)
    copy.start()
    copy.wait()
    slot = pl.ds(pl.multiple_of(at_ref[2] * SLICE, SLICE), SLICE)
    for t in range(STEPS - 1):
        for out_ref, part in ((theirs_ref, 1 - core), (mine_ref, core)):
            turned_ref[...] = held_ref[t, pl.ds(pl.multiple_of(part * HALF, 16), HALF), :].T
            out_ref[t] = turned_ref[slot, :]


def rows(at, rates):
    shape = jax.ShapeDtypeStruct((STEPS - 1, SLICE, HALF), jnp.bfloat16)
    return pl.pallas_call(
        rows_kernel,
        in_specs=[SMEM, HBM],
        out_specs=[VMEM, VMEM],
        out_shape=[shape, shape],
        scratch_shapes=[
            pltpu.VMEM((STEPS - 1, QUARTER, TRIALS), jnp.bfloat16),
            pltpu.VMEM((TRIALS, HALF), jnp.bfloat16),
            pltpu.SemaphoreType.DMA,
        ],
        cost_estimate=cost(0, 600_000),
        compiler_params=params(ROWS),
        name="rows",
    )(at, rates)


def fill(at_ref, first_ref, second_ref, g_ref):
    core, x = at_ref[1], at_ref[3]
    for ref, part in ((first_ref, core), (second_ref, 1 - core)):
        if ref.shape == (TRIALS, HALF):
            g_ref[:, half(part)] = ref[...]
        else:
            for j in range(2):
                slot = (x + 2 * X - j - 2 * part) % X
                g_ref[pl.ds(pl.multiple_of(slot * SLICE, SLICE), SLICE), :] = ref[j]


def back_kernel(at_ref, first_ref, second_ref, mine_ref, theirs_ref, out_ref, g_ref, held_ref, sems):
    core = at_ref[1]
    copies = [
        pltpu.make_async_copy(theirs_ref.at[q], held_ref.at[q], sems.at[q]) for q in range(4)
    ]
    for copy in copies:
        copy.start()
    fill(at_ref, first_ref, second_ref, g_ref)
    for ref, block in ((mine_ref, core), (held_ref, 1 - core)):
        for q in range(4):
            if ref is held_ref:
                copies[q].wait()
            got = jnp.dot(g_ref[...], ref[q], preferred_element_type=jnp.float32)
            got = got.astype(jnp.bfloat16)
            for part in range(Y):
                out_ref[part, block * 4 + q] = got[part * SLICE : (part + 1) * SLICE]


def back(at, pair, mine, theirs):
    return pl.pallas_call(
        back_kernel,
        in_specs=[SMEM, VMEM, VMEM, VMEM, HBM],
        out_specs=[VMEM, VMEM],
        out_shape=[
            jax.ShapeDtypeStruct((Y, 8, SLICE, HALF), jnp.bfloat16),
            jax.ShapeDtypeStruct((TRIALS, QUARTER), jnp.bfloat16),
        ],
        scratch_shapes=[
            pltpu.VMEM((4, QUARTER, HALF), jnp.bfloat16),
            pltpu.SemaphoreType.DMA((4,)),
        ],
        cost_estimate=cost(2 * TRIALS * QUARTER * COLS, 6_000_000),
        compiler_params=params(BACK),
        name="back",
    )(at, *pair, mine, theirs)


TILE = 512
TILES = COLS // TILE


def outer_kernel(
    at_ref, g4, g3, g2, first_ref, second_ref, rates_ref, out_ref, g_ref, turned_ref, held_ref, done_ref, sems
):
    def came(j):
        columns = pl.ds(j * TILE, TILE)
        return pltpu.make_async_copy(rates_ref.at[0:STEPS, columns], held_ref.at[:, columns], sems.at[0, j])

    def went(j):
        columns = pl.ds(j * TILE, TILE)
        return pltpu.make_async_copy(done_ref.at[j], out_ref.at[:, columns], sems.at[1, j])

    for j in range(TILES):
        came(j).start()
    for t, ref in ((3, g4), (2, g3), (1, g2)):
        turned_ref[:, t * TRIALS : (t + 1) * TRIALS] = ref[...].T
    fill(at_ref, first_ref, second_ref, g_ref)
    turned_ref[:, :TRIALS] = g_ref[...].T
    for j in range(TILES):
        came(j).wait()
        columns = slice(j * TILE, (j + 1) * TILE)
        before = jnp.concatenate([held_ref[t, columns, :] for t in range(STEPS)], axis=1)
        done_ref[j] = lax.dot_general(
            turned_ref[...], before, (((1,), (1,)), ((), ())), preferred_element_type=jnp.float32
        ).astype(jnp.bfloat16)
        went(j).start()
    for j in range(TILES):
        went(j).wait()


def outer(at, full, pair, rates):
    return pl.pallas_call(
        outer_kernel,
        in_specs=[SMEM] + [VMEM] * 5 + [HBM],
        out_specs=HBM,
        out_shape=jax.ShapeDtypeStruct((QUARTER, COLS), jnp.bfloat16),
        scratch_shapes=[
            pltpu.VMEM((TRIALS, QUARTER), jnp.bfloat16),
            pltpu.VMEM((QUARTER, STEPS * TRIALS), jnp.bfloat16),
            pltpu.VMEM((STEPS, COLS, TRIALS), jnp.bfloat16),
            pltpu.VMEM((TILES, QUARTER, TILE), jnp.bfloat16),
            pltpu.SemaphoreType.DMA((2, TILES)),
        ],
        cost_estimate=cost(2 * STEPS * TRIALS * QUARTER * COLS, 8_000_000),
        compiler_params=params(OUTER),
        name="outer",
    )(at, *full, *pair, rates)


def whole(weights, rates):
    y, z, x, core = (lax.axis_index(a) for a in EVERY)
    at = jnp.stack([z % 4, core, y, x]).astype(jnp.int32)

    def swapped(array):
        return lax.ppermute(array, "core", SWAP)

    def of_root_core(mine, theirs):
        return jnp.where(core == z // 4, mine, swapped(theirs))

    root = of_root_core(*first(at, rates))
    parts = [lax.ppermute(root, EVERY, from_root(shift)) for shift in (1, 2, 3)]
    own = jnp.where(x == y, root, parts[0] + parts[1] + parts[2])
    late_weights, late_rates, _ = lax.optimization_barrier((weights, rates, root))
    theirs = swapped(split(at, late_weights, True))
    mine = split(at, late_weights, False)
    before = of_root_core(*rows(at, late_rates))
    pair = (own, swapped(own))
    full = []
    for step in range(STEPS - 1, 0, -1):
        sums, whole_grad = back(at, pair, mine, theirs)
        full.append(whole_grad)
        sums = lax.all_to_all(sums.reshape(Y * Z, SLICE, HALF), ("y", "z"), 0, 0, tiled=True)
        sums = jnp.sum(sums.astype(jnp.float32), axis=0)
        rate = before[step - 1].astype(jnp.float32)
        share = (sums * (1.0 - rate * rate)).astype(jnp.bfloat16)
        other = swapped(share)
        share = jnp.where(
            core == 0, jnp.concatenate([share, other], 1), jnp.concatenate([other, share], 1)
        )
        slices = jnp.stack([lax.ppermute(share, EVERY, across(j)) for j in range(2)])
        pair = (slices, swapped(slices))
    return outer(at, full, pair, rates)


def solution(mesh):
    fine = Mesh(mesh.devices.reshape(Y, Z, X, C), EVERY)
    in_specs = (P(("y", "z"), ("x", "core")), P(None, ("x", "core"), None))
    out_specs = P(("y", "z"), ("x", "core"))
    return jax.shard_map(whole, mesh=fine, in_specs=in_specs, out_specs=out_specs, check_vma=False)
```

```python
import functools

import jax
import jax.numpy as jnp
from jax import lax
from jax.experimental import pallas as pl
from jax.experimental.pallas import tpu as pltpu
from jax.sharding import Mesh, PartitionSpec as P

STEPS = 4
Y, Z, X, C = 4, 8, 4, 2
EVERY = ("y", "z", "x", "core")
SWAP = [(0, 1), (1, 0)]
HALF = 384
QUARTER = 768
TRIALS = 128
SLICE = 32
SPLIT, ROWS, BACK, OUTER, KEEP = 48, 52, 8, 52, 48
COLS = 3072
VMEM = pl.BlockSpec(memory_space=pltpu.VMEM)
SMEM = pl.BlockSpec(memory_space=pltpu.SMEM)
HBM = pl.BlockSpec(memory_space=pltpu.HBM)


def flat(y, z, x, core):
    return ((y % Y * Z + z) * X + x % X) * C + core


def across(j):
    return [
        (flat(y, z, x, core), flat(x, z, y + 2 * j + core, core))
        for y in range(Y) for z in range(Z) for x in range(X) for core in range(C)
    ]


def from_root(shift):
    return [(flat(y, z, y, z // 4), flat(y, z, y + shift, z // 4)) for y in range(Y) for z in range(Z)]


def params(mib):
    return pltpu.CompilerParams(vmem_limit_bytes=mib << 20)


def cost(flops, moved):
    return pl.CostEstimate(flops=flops, bytes_accessed=moved, transcendentals=0)


def first_kernel(at_ref, rates_ref, out_ref, last_ref, zero_ref, sems):
    rows = pl.ds(pl.multiple_of(at_ref[0] * QUARTER, 16), QUARTER)
    copies = [
        pltpu.make_async_copy(rates_ref.at[STEPS, rows], last_ref, sems.at[0]),
        pltpu.make_async_copy(rates_ref.at[0, rows], zero_ref, sems.at[1]),
    ]
    for copy in copies:
        copy.start()
    for copy in copies:
        copy.wait()
    last = last_ref[...].astype(jnp.float32)
    zero = zero_ref[...].astype(jnp.float32)
    out_ref[...] = ((last - zero) * (1.0 - last * last)).astype(jnp.bfloat16).T


def first(at, rates):
    return pl.pallas_call(
        first_kernel,
        in_specs=[SMEM, HBM],
        out_specs=VMEM,
        out_shape=jax.ShapeDtypeStruct((TRIALS, QUARTER), jnp.bfloat16),
        scratch_shapes=[
            pltpu.VMEM((QUARTER, TRIALS), jnp.bfloat16),
            pltpu.VMEM((QUARTER, TRIALS), jnp.bfloat16),
            pltpu.SemaphoreType.DMA((2,)),
        ],
        compiler_params=params(52),
        name="first",
    )(at, rates)


def split_kernel(at_ref, w_ref, out_ref, sems, *, partner):
    part = 1 - at_ref[1] if partner else at_ref[1]
    copies = []
    for q in range(4):
        columns = pl.ds(pl.multiple_of((2 * q + part) * HALF, 128), HALF)
        copies.append(pltpu.make_async_copy(w_ref.at[:, columns], out_ref.at[q], sems.at[q]))
    for copy in copies:
        copy.start()
    for copy in copies:
        copy.wait()


def split(at, weights, partner):
    return pl.pallas_call(
        functools.partial(split_kernel, partner=partner),
        in_specs=[SMEM, HBM],
        out_specs=VMEM,
        out_shape=jax.ShapeDtypeStruct((4, QUARTER, HALF), jnp.bfloat16),
        scratch_shapes=[pltpu.SemaphoreType.DMA((4,))],
        cost_estimate=cost(0, 4_718_592),
        compiler_params=params(SPLIT if partner else KEEP),
        name="split",
    )(at, weights)


def rows_kernel(at_ref, rates_ref, mine_ref, theirs_ref, held_ref, turned_ref, sem):
    core = at_ref[1]
    rows = pl.ds(pl.multiple_of(at_ref[0] * QUARTER, 16), QUARTER)
    copy = pltpu.make_async_copy(rates_ref.at[1:STEPS, rows], held_ref, sem)
    copy.start()
    copy.wait()
    slot = pl.ds(pl.multiple_of(at_ref[2] * SLICE, SLICE), SLICE)
    for t in range(STEPS - 1):
        for out_ref, part in ((theirs_ref, 1 - core), (mine_ref, core)):
            turned_ref[...] = held_ref[t, pl.ds(pl.multiple_of(part * HALF, 16), HALF), :].T
            out_ref[t] = turned_ref[slot, :]


def rows(at, rates):
    shape = jax.ShapeDtypeStruct((STEPS - 1, SLICE, HALF), jnp.bfloat16)
    return pl.pallas_call(
        rows_kernel,
        in_specs=[SMEM, HBM],
        out_specs=[VMEM, VMEM],
        out_shape=[shape, shape],
        scratch_shapes=[
            pltpu.VMEM((STEPS - 1, QUARTER, TRIALS), jnp.bfloat16),
            pltpu.VMEM((TRIALS, HALF), jnp.bfloat16),
            pltpu.SemaphoreType.DMA,
        ],
        cost_estimate=cost(0, 600_000),
        compiler_params=params(ROWS),
        name="rows",
    )(at, rates)


def fill(at_ref, pair_refs, g_ref):
    core, x = at_ref[1], at_ref[3]
    if len(pair_refs) == 1:
        g_ref[...] = pair_refs[0][...]
        return
    for ref, part in zip(pair_refs, (core, 1 - core)):
        for j in range(2):
            slot = (x + 2 * X - 2 * j - part) % X
            g_ref[pl.ds(pl.multiple_of(slot * SLICE, SLICE), SLICE), :] = ref[j]


def back_kernel(at_ref, *refs):
    *pair_refs, mine_ref, theirs_ref, out_ref, g_ref, held_ref, sems = refs
    core = at_ref[1]
    copies = [
        pltpu.make_async_copy(theirs_ref.at[q], held_ref.at[q], sems.at[q]) for q in range(4)
    ]
    for copy in copies:
        copy.start()
    fill(at_ref, pair_refs, g_ref)
    for ref, block in ((mine_ref, core), (held_ref, 1 - core)):
        for q in range(4):
            if ref is held_ref:
                copies[q].wait()
            got = jnp.dot(g_ref[...], ref[q], preferred_element_type=jnp.float32)
            got = got.astype(jnp.bfloat16)
            for part in range(Y):
                out_ref[part, block * 4 + q] = got[part * SLICE : (part + 1) * SLICE]


def back(at, pair, mine, theirs):
    return pl.pallas_call(
        back_kernel,
        in_specs=[SMEM] + [VMEM] * len(pair) + [VMEM, HBM],
        out_specs=[VMEM, VMEM],
        out_shape=[
            jax.ShapeDtypeStruct((Y, 8, SLICE, HALF), jnp.bfloat16),
            jax.ShapeDtypeStruct((TRIALS, QUARTER), jnp.bfloat16),
        ],
        scratch_shapes=[
            pltpu.VMEM((4, QUARTER, HALF), jnp.bfloat16),
            pltpu.SemaphoreType.DMA((4,)),
        ],
        cost_estimate=cost(2 * TRIALS * QUARTER * COLS, 6_000_000),
        compiler_params=params(BACK),
        name="back",
    )(at, *pair, mine, theirs)


TILE = 512
TILES = COLS // TILE


def outer_kernel(
    at_ref, g4, g3, g2, first_ref, second_ref, rates_ref, out_ref, g_ref, turned_ref, held_ref, done_ref, sems
):
    def came(j):
        columns = pl.ds(j * TILE, TILE)
        return pltpu.make_async_copy(rates_ref.at[0:STEPS, columns], held_ref.at[:, columns], sems.at[0, j])

    def went(j):
        columns = pl.ds(j * TILE, TILE)
        return pltpu.make_async_copy(done_ref.at[j], out_ref.at[:, columns], sems.at[1, j])

    for j in range(TILES):
        came(j).start()
    for t, ref in ((3, g4), (2, g3), (1, g2)):
        turned_ref[:, t * TRIALS : (t + 1) * TRIALS] = ref[...].T
    fill(at_ref, (first_ref, second_ref), g_ref)
    turned_ref[:, :TRIALS] = g_ref[...].T
    for j in range(TILES):
        came(j).wait()
        columns = slice(j * TILE, (j + 1) * TILE)
        before = jnp.concatenate([held_ref[t, columns, :] for t in range(STEPS)], axis=1)
        done_ref[j] = lax.dot_general(
            turned_ref[...], before, (((1,), (1,)), ((), ())), preferred_element_type=jnp.float32
        ).astype(jnp.bfloat16)
        went(j).start()
    for j in range(TILES):
        went(j).wait()


def outer(at, full, pair, rates):
    return pl.pallas_call(
        outer_kernel,
        in_specs=[SMEM] + [VMEM] * 5 + [HBM],
        out_specs=HBM,
        out_shape=jax.ShapeDtypeStruct((QUARTER, COLS), jnp.bfloat16),
        scratch_shapes=[
            pltpu.VMEM((TRIALS, QUARTER), jnp.bfloat16),
            pltpu.VMEM((QUARTER, STEPS * TRIALS), jnp.bfloat16),
            pltpu.VMEM((STEPS, COLS, TRIALS), jnp.bfloat16),
            pltpu.VMEM((TILES, QUARTER, TILE), jnp.bfloat16),
            pltpu.SemaphoreType.DMA((2, TILES)),
        ],
        cost_estimate=cost(2 * STEPS * TRIALS * QUARTER * COLS, 8_000_000),
        compiler_params=params(OUTER),
        name="outer",
    )(at, *full, *pair, rates)


def whole(weights, rates):
    y, z, x, core = (lax.axis_index(a) for a in EVERY)
    at = jnp.stack([z % 4, core, y, x]).astype(jnp.int32)

    def swapped(array):
        return lax.ppermute(array, "core", SWAP)

    is_root_core = core == z // 4
    root = first(at, rates)
    parts = [lax.ppermute(root, EVERY, from_root(shift)) for shift in (1, 2, 3)]
    late_weights, late_rates, _ = lax.optimization_barrier((weights, rates, root))
    theirs = swapped(split(at, late_weights, True))
    mine = split(at, late_weights, False)
    before, other = rows(at, late_rates)
    before = jnp.where(is_root_core, before, swapped(other))
    came = jnp.where(x == y, root, parts[0] + parts[1] + parts[2])
    grad, before = lax.optimization_barrier(
        (jnp.where(is_root_core, came, swapped(came)), before)
    )
    pair = (grad,)
    full = []
    for step in range(STEPS - 1, 0, -1):
        sums, whole_grad = back(at, pair, mine, theirs)
        full.append(whole_grad)
        sums = lax.all_to_all(sums.reshape(Y * Z, SLICE, HALF), ("y", "z"), 0, 0, tiled=True)
        sums = jnp.sum(sums.astype(jnp.float32), axis=0)
        rate = before[step - 1].astype(jnp.float32)
        share = (sums * (1.0 - rate * rate)).astype(jnp.bfloat16)
        other = swapped(share)
        share = jnp.where(
            core == 0, jnp.concatenate([share, other], 1), jnp.concatenate([other, share], 1)
        )
        slices = jnp.stack([lax.ppermute(share, EVERY, across(j)) for j in range(2)])
        pair = (slices, swapped(slices))
    return outer(at, full, pair, rates)


def solution(mesh):
    fine = Mesh(mesh.devices.reshape(Y, Z, X, C), EVERY)
    in_specs = (P(("y", "z"), ("x", "core")), P(None, ("x", "core"), None))
    out_specs = P(("y", "z"), ("x", "core"))
    return jax.shard_map(whole, mesh=fine, in_specs=in_specs, out_specs=out_specs, check_vma=False)
```

```python
import jax
import jax.numpy as jnp
from jax import lax
from jax.experimental import pallas as pl
from jax.experimental.pallas import tpu as pltpu
from jax.sharding import Mesh, PartitionSpec as P

STEPS = 4
Y, Z, X, C = 4, 8, 4, 2
EVERY = ("y", "z", "x", "core")
SWAP = [(0, 1), (1, 0)]
HALF = 384
QUARTER = 768
TRIALS = 128
SLICE = 32
FIRST, BACK, OUTER, KEEP = 52, 8, 52, 48
COLS = 3072
VMEM = pl.BlockSpec(memory_space=pltpu.VMEM)
SMEM = pl.BlockSpec(memory_space=pltpu.SMEM)
HBM = pl.BlockSpec(memory_space=pltpu.HBM)


def flat(y, z, x, core):
    return ((y % Y * Z + z) * X + x % X) * C + core


def across(j):
    return [
        (flat(y, z, x, core), flat(x, z, y + 2 * j + core, core))
        for y in range(Y) for z in range(Z) for x in range(X) for core in range(C)
    ]


def from_root(shift):
    return [(flat(y, z, y, z // 4), flat(y, z, y + shift, z // 4)) for y in range(Y) for z in range(Z)]


def params(mib):
    return pltpu.CompilerParams(vmem_limit_bytes=mib << 20)


def cost(flops, moved):
    return pl.CostEstimate(flops=flops, bytes_accessed=moved, transcendentals=0)


def first_kernel(at_ref, rates_ref, out_ref, mine_ref, theirs_ref, last_ref, zero_ref, held_ref, turned_ref, sems):
    core = at_ref[1]
    rows = pl.ds(pl.multiple_of(at_ref[0] * QUARTER, 16), QUARTER)
    copies = [
        pltpu.make_async_copy(rates_ref.at[STEPS, rows], last_ref, sems.at[0]),
        pltpu.make_async_copy(rates_ref.at[0, rows], zero_ref, sems.at[1]),
        pltpu.make_async_copy(rates_ref.at[1:STEPS, rows], held_ref, sems.at[2]),
    ]
    for copy in copies:
        copy.start()
    copies[0].wait()
    copies[1].wait()
    last = last_ref[...].astype(jnp.float32)
    zero = zero_ref[...].astype(jnp.float32)
    out_ref[...] = ((last - zero) * (1.0 - last * last)).astype(jnp.bfloat16).T
    copies[2].wait()
    slot = pl.ds(pl.multiple_of(at_ref[2] * SLICE, SLICE), SLICE)
    for t in range(STEPS - 1):
        turned_ref[...] = held_ref[t].T
        for ref, part in ((theirs_ref, 1 - core), (mine_ref, core)):
            ref[t] = turned_ref[slot, pl.ds(pl.multiple_of(part * HALF, 128), HALF)]


def first(at, rates):
    small = jax.ShapeDtypeStruct((STEPS - 1, SLICE, HALF), jnp.bfloat16)
    return pl.pallas_call(
        first_kernel,
        in_specs=[SMEM, HBM],
        out_specs=[VMEM] * 3,
        out_shape=[jax.ShapeDtypeStruct((TRIALS, QUARTER), jnp.bfloat16), small, small],
        scratch_shapes=[
            pltpu.VMEM((QUARTER, TRIALS), jnp.bfloat16),
            pltpu.VMEM((QUARTER, TRIALS), jnp.bfloat16),
            pltpu.VMEM((STEPS - 1, QUARTER, TRIALS), jnp.bfloat16),
            pltpu.VMEM((TRIALS, QUARTER), jnp.bfloat16),
            pltpu.SemaphoreType.DMA((3,)),
        ],
        compiler_params=params(FIRST),
        name="first",
    )(at, rates)


def split_kernel(at_ref, w_ref, mine_ref, theirs_ref, held_ref, sems):
    core = at_ref[1]

    def columns(q, part):
        return pl.ds(pl.multiple_of((2 * q + part) * HALF, 128), HALF)

    took = [
        pltpu.make_async_copy(w_ref.at[:, columns(q, 1 - core)], held_ref.at[q], sems.at[0, q])
        for q in range(4)
    ]
    kept = [
        pltpu.make_async_copy(w_ref.at[:, columns(q, core)], mine_ref.at[q], sems.at[1, q])
        for q in range(4)
    ]
    gave = [pltpu.make_async_copy(held_ref.at[q], theirs_ref.at[q], sems.at[2, q]) for q in range(4)]
    for copy in took + kept:
        copy.start()
    for q in range(4):
        took[q].wait()
        gave[q].start()
    for copy in kept + gave:
        copy.wait()


def split(at, weights):
    shape = jax.ShapeDtypeStruct((4, QUARTER, HALF), jnp.bfloat16)
    return pl.pallas_call(
        split_kernel,
        in_specs=[SMEM, HBM],
        out_specs=[VMEM, HBM],
        out_shape=[shape, shape],
        scratch_shapes=[
            pltpu.VMEM((4, QUARTER, HALF), jnp.bfloat16),
            pltpu.SemaphoreType.DMA((3, 4)),
        ],
        cost_estimate=cost(0, 9_437_184),
        compiler_params=params(KEEP),
        name="split",
    )(at, weights)


def fill(at_ref, pair_refs, g_ref):
    core, x = at_ref[1], at_ref[3]
    if len(pair_refs) == 1:
        g_ref[...] = pair_refs[0][...]
        return
    for ref, part in zip(pair_refs, (core, 1 - core)):
        for j in range(2):
            slot = (x + 2 * X - 2 * j - part) % X
            g_ref[pl.ds(pl.multiple_of(slot * SLICE, SLICE), SLICE), :] = ref[j]


def back_kernel(at_ref, *refs):
    *pair_refs, mine_ref, theirs_ref, out_ref, g_ref, held_ref, sems = refs
    core = at_ref[1]
    copies = [
        pltpu.make_async_copy(theirs_ref.at[q], held_ref.at[q], sems.at[q]) for q in range(4)
    ]
    for copy in copies:
        copy.start()
    fill(at_ref, pair_refs, g_ref)
    for ref, block in ((mine_ref, core), (held_ref, 1 - core)):
        for q in range(4):
            if ref is held_ref:
                copies[q].wait()
            got = jnp.dot(g_ref[...], ref[q], preferred_element_type=jnp.float32)
            got = got.astype(jnp.bfloat16)
            for part in range(Y):
                out_ref[part, block * 4 + q] = got[part * SLICE : (part + 1) * SLICE]


def back(at, pair, mine, theirs):
    return pl.pallas_call(
        back_kernel,
        in_specs=[SMEM] + [VMEM] * len(pair) + [VMEM, HBM],
        out_specs=[VMEM, VMEM],
        out_shape=[
            jax.ShapeDtypeStruct((Y, 8, SLICE, HALF), jnp.bfloat16),
            jax.ShapeDtypeStruct((TRIALS, QUARTER), jnp.bfloat16),
        ],
        scratch_shapes=[
            pltpu.VMEM((4, QUARTER, HALF), jnp.bfloat16),
            pltpu.SemaphoreType.DMA((4,)),
        ],
        cost_estimate=cost(2 * TRIALS * QUARTER * COLS, 6_000_000),
        compiler_params=params(BACK),
        name="back",
    )(at, *pair, mine, theirs)


TILE = 512
TILES = COLS // TILE


def outer_kernel(
    at_ref, g4, g3, g2, first_ref, second_ref, rates_ref, out_ref, g_ref, turned_ref, held_ref, done_ref, sems
):
    def came(j):
        columns = pl.ds(j * TILE, TILE)
        return pltpu.make_async_copy(rates_ref.at[0:STEPS, columns], held_ref.at[:, columns], sems.at[0, j])

    def went(j):
        columns = pl.ds(j * TILE, TILE)
        return pltpu.make_async_copy(done_ref.at[j], out_ref.at[:, columns], sems.at[1, j])

    for j in range(TILES):
        came(j).start()
    for t, ref in ((3, g4), (2, g3), (1, g2)):
        turned_ref[:, t * TRIALS : (t + 1) * TRIALS] = ref[...].T
    fill(at_ref, (first_ref, second_ref), g_ref)
    turned_ref[:, :TRIALS] = g_ref[...].T
    for j in range(TILES):
        came(j).wait()
        columns = slice(j * TILE, (j + 1) * TILE)
        before = jnp.concatenate([held_ref[t, columns, :] for t in range(STEPS)], axis=1)
        done_ref[j] = lax.dot_general(
            turned_ref[...], before, (((1,), (1,)), ((), ())), preferred_element_type=jnp.float32
        ).astype(jnp.bfloat16)
        went(j).start()
    for j in range(TILES):
        went(j).wait()


def outer(at, full, pair, rates):
    return pl.pallas_call(
        outer_kernel,
        in_specs=[SMEM] + [VMEM] * 5 + [HBM],
        out_specs=HBM,
        out_shape=jax.ShapeDtypeStruct((QUARTER, COLS), jnp.bfloat16),
        scratch_shapes=[
            pltpu.VMEM((TRIALS, QUARTER), jnp.bfloat16),
            pltpu.VMEM((QUARTER, STEPS * TRIALS), jnp.bfloat16),
            pltpu.VMEM((STEPS, COLS, TRIALS), jnp.bfloat16),
            pltpu.VMEM((TILES, QUARTER, TILE), jnp.bfloat16),
            pltpu.SemaphoreType.DMA((2, TILES)),
        ],
        cost_estimate=cost(2 * STEPS * TRIALS * QUARTER * COLS, 8_000_000),
        compiler_params=params(OUTER),
        name="outer",
    )(at, *full, *pair, rates)


def whole(weights, rates):
    y, z, x, core = (lax.axis_index(a) for a in EVERY)
    at = jnp.stack([z % 4, core, y, x]).astype(jnp.int32)

    def swapped(array):
        return lax.ppermute(array, "core", SWAP)

    is_root_core = core == z // 4
    root, before, other = first(at, rates)
    parts = [lax.ppermute(root, EVERY, from_root(shift)) for shift in (1, 2, 3)]
    mine, theirs = split(at, lax.optimization_barrier((weights, root))[0])
    theirs = swapped(theirs)
    before = jnp.where(is_root_core, before, swapped(other))
    came = jnp.where(x == y, root, parts[0] + parts[1] + parts[2])
    grad, before = lax.optimization_barrier(
        (jnp.where(is_root_core, came, swapped(came)), before)
    )
    pair = (grad,)
    full = []
    for step in range(STEPS - 1, 0, -1):
        sums, whole_grad = back(at, pair, mine, theirs)
        full.append(whole_grad)
        sums = lax.all_to_all(sums.reshape(Y * Z, SLICE, HALF), ("y", "z"), 0, 0, tiled=True)
        sums = jnp.sum(sums.astype(jnp.float32), axis=0)
        rate = before[step - 1].astype(jnp.float32)
        share = (sums * (1.0 - rate * rate)).astype(jnp.bfloat16)
        other = swapped(share)
        share = jnp.where(
            core == 0, jnp.concatenate([share, other], 1), jnp.concatenate([other, share], 1)
        )
        slices = jnp.stack([lax.ppermute(share, EVERY, across(j)) for j in range(2)])
        pair = (slices, swapped(slices))
    return outer(at, full, pair, rates)


def solution(mesh):
    fine = Mesh(mesh.devices.reshape(Y, Z, X, C), EVERY)
    in_specs = (P(("y", "z"), ("x", "core")), P(None, ("x", "core"), None))
    out_specs = P(("y", "z"), ("x", "core"))
    return jax.shard_map(whole, mesh=fine, in_specs=in_specs, out_specs=out_specs, check_vma=False)
```

```python
import jax
import jax.numpy as jnp
from jax import lax
from jax.experimental import pallas as pl
from jax.experimental.pallas import tpu as pltpu
from jax.sharding import Mesh, PartitionSpec as P

STEPS = 4
Y, Z, X, C = 4, 8, 4, 2
EVERY = ("y", "z", "x", "core")
SWAP = [(0, 1), (1, 0)]
HALF = 384
QUARTER = 768
TRIALS = 128
SLICE = 32
FIRST, BACK, OUTER, KEEP = 52, 8, 24, 48
COLS = 3072
VMEM = pl.BlockSpec(memory_space=pltpu.VMEM)
SMEM = pl.BlockSpec(memory_space=pltpu.SMEM)
HBM = pl.BlockSpec(memory_space=pltpu.HBM)


def flat(y, z, x, core):
    return ((y % Y * Z + z) * X + x % X) * C + core


def across(j):
    return [
        (flat(y, z, x, core), flat(x, z, y + 2 * j + core, core))
        for y in range(Y) for z in range(Z) for x in range(X) for core in range(C)
    ]


def from_root(shift):
    return [(flat(y, z, y, z // 4), flat(y, z, y + shift, z // 4)) for y in range(Y) for z in range(Z)]


def params(mib):
    return pltpu.CompilerParams(vmem_limit_bytes=mib << 20)


def cost(flops, moved):
    return pl.CostEstimate(flops=flops, bytes_accessed=moved, transcendentals=0)


def first_kernel(at_ref, rates_ref, out_ref, mine_ref, theirs_ref, last_ref, zero_ref, held_ref, turned_ref, sems):
    core = at_ref[1]
    rows = pl.ds(pl.multiple_of(at_ref[0] * QUARTER, 16), QUARTER)
    copies = [
        pltpu.make_async_copy(rates_ref.at[STEPS, rows], last_ref, sems.at[0]),
        pltpu.make_async_copy(rates_ref.at[0, rows], zero_ref, sems.at[1]),
        pltpu.make_async_copy(rates_ref.at[1:STEPS, rows], held_ref, sems.at[2]),
    ]
    for copy in copies:
        copy.start()
    copies[0].wait()
    copies[1].wait()
    last = last_ref[...].astype(jnp.float32)
    zero = zero_ref[...].astype(jnp.float32)
    out_ref[...] = ((last - zero) * (1.0 - last * last)).astype(jnp.bfloat16).T
    copies[2].wait()
    slot = pl.ds(pl.multiple_of(at_ref[2] * SLICE, SLICE), SLICE)
    for t in range(STEPS - 1):
        turned_ref[...] = held_ref[t].T
        for ref, part in ((theirs_ref, 1 - core), (mine_ref, core)):
            ref[t] = turned_ref[slot, pl.ds(pl.multiple_of(part * HALF, 128), HALF)]


def first(at, rates):
    small = jax.ShapeDtypeStruct((STEPS - 1, SLICE, HALF), jnp.bfloat16)
    return pl.pallas_call(
        first_kernel,
        in_specs=[SMEM, HBM],
        out_specs=[VMEM] * 3,
        out_shape=[jax.ShapeDtypeStruct((TRIALS, QUARTER), jnp.bfloat16), small, small],
        scratch_shapes=[
            pltpu.VMEM((QUARTER, TRIALS), jnp.bfloat16),
            pltpu.VMEM((QUARTER, TRIALS), jnp.bfloat16),
            pltpu.VMEM((STEPS - 1, QUARTER, TRIALS), jnp.bfloat16),
            pltpu.VMEM((TRIALS, QUARTER), jnp.bfloat16),
            pltpu.SemaphoreType.DMA((3,)),
        ],
        compiler_params=params(FIRST),
        name="first",
    )(at, rates)


def columns(q, part):
    return pl.ds(pl.multiple_of((2 * q + part) * HALF, 128), HALF)


def give_kernel(at_ref, w_ref, theirs_ref, held_ref, sems):
    took = [
        pltpu.make_async_copy(w_ref.at[:, columns(q, 1 - at_ref[1])], held_ref.at[q], sems.at[0, q])
        for q in range(4)
    ]
    gave = [pltpu.make_async_copy(held_ref.at[q], theirs_ref.at[q], sems.at[1, q]) for q in range(4)]
    for copy in took:
        copy.start()
    for q in range(4):
        took[q].wait()
        gave[q].start()
    for copy in gave:
        copy.wait()


def give(at, weights):
    return pl.pallas_call(
        give_kernel,
        in_specs=[SMEM, HBM],
        out_specs=HBM,
        out_shape=jax.ShapeDtypeStruct((4, QUARTER, HALF), jnp.bfloat16),
        scratch_shapes=[
            pltpu.VMEM((4, QUARTER, HALF), jnp.bfloat16),
            pltpu.SemaphoreType.DMA((2, 4)),
        ],
        cost_estimate=cost(0, 4_718_592),
        compiler_params=params(52),
        name="give",
    )(at, weights)


def keep_kernel(at_ref, w_ref, mine_ref, sems):
    copies = [
        pltpu.make_async_copy(w_ref.at[:, columns(q, at_ref[1])], mine_ref.at[q], sems.at[q])
        for q in range(4)
    ]
    for copy in copies:
        copy.start()
    for copy in copies:
        copy.wait()


def keep(at, weights):
    return pl.pallas_call(
        keep_kernel,
        in_specs=[SMEM, HBM],
        out_specs=VMEM,
        out_shape=jax.ShapeDtypeStruct((4, QUARTER, HALF), jnp.bfloat16),
        scratch_shapes=[pltpu.SemaphoreType.DMA((4,))],
        cost_estimate=cost(0, 4_718_592),
        compiler_params=params(KEEP),
        name="keep",
    )(at, weights)


def fill(at_ref, pair_refs, g_ref):
    core, x = at_ref[1], at_ref[3]
    if len(pair_refs) == 1:
        g_ref[...] = pair_refs[0][...]
        return
    for ref, part in zip(pair_refs, (core, 1 - core)):
        for j in range(2):
            slot = (x + 2 * X - 2 * j - part) % X
            g_ref[pl.ds(pl.multiple_of(slot * SLICE, SLICE), SLICE), :] = ref[j]


def back_kernel(at_ref, *refs):
    *pair_refs, mine_ref, theirs_ref, out_ref, g_ref, held_ref, sems = refs
    core = at_ref[1]
    copies = [
        pltpu.make_async_copy(theirs_ref.at[q], held_ref.at[q], sems.at[q]) for q in range(4)
    ]
    for copy in copies:
        copy.start()
    fill(at_ref, pair_refs, g_ref)
    for ref, block in ((mine_ref, core), (held_ref, 1 - core)):
        for q in range(4):
            if ref is held_ref:
                copies[q].wait()
            got = jnp.dot(g_ref[...], ref[q], preferred_element_type=jnp.float32)
            got = got.astype(jnp.bfloat16)
            for part in range(Y):
                out_ref[part, block * 4 + q] = got[part * SLICE : (part + 1) * SLICE]


def back(at, pair, mine, theirs):
    return pl.pallas_call(
        back_kernel,
        in_specs=[SMEM] + [VMEM] * len(pair) + [VMEM, HBM],
        out_specs=[VMEM, VMEM],
        out_shape=[
            jax.ShapeDtypeStruct((Y, 8, SLICE, HALF), jnp.bfloat16),
            jax.ShapeDtypeStruct((TRIALS, QUARTER), jnp.bfloat16),
        ],
        scratch_shapes=[
            pltpu.VMEM((4, QUARTER, HALF), jnp.bfloat16),
            pltpu.SemaphoreType.DMA((4,)),
        ],
        cost_estimate=cost(2 * TRIALS * QUARTER * COLS, 6_000_000),
        compiler_params=params(BACK),
        name="back",
    )(at, *pair, mine, theirs)


TILE = 512
TILES = COLS // TILE


def outer_kernel(
    at_ref, g4, g3, g2, first_ref, second_ref, rates_ref, out_ref, g_ref, turned_ref, done_ref, sems
):
    went = [
        pltpu.make_async_copy(done_ref.at[j], out_ref.at[:, pl.ds(j * TILE, TILE)], sems.at[j])
        for j in range(TILES)
    ]
    for t, ref in ((3, g4), (2, g3), (1, g2)):
        turned_ref[:, t * TRIALS : (t + 1) * TRIALS] = ref[...].T
    fill(at_ref, (first_ref, second_ref), g_ref)
    turned_ref[:, :TRIALS] = g_ref[...].T
    for j in range(TILES):
        part = slice(j * TILE, (j + 1) * TILE)
        before = jnp.concatenate([rates_ref[t, part, :] for t in range(STEPS)], axis=1)
        done_ref[j] = lax.dot_general(
            turned_ref[...], before, (((1,), (1,)), ((), ())), preferred_element_type=jnp.float32
        ).astype(jnp.bfloat16)
        went[j].start()
    for copy in went:
        copy.wait()


def outer(at, full, pair, rates):
    return pl.pallas_call(
        outer_kernel,
        in_specs=[SMEM] + [VMEM] * 6,
        out_specs=HBM,
        out_shape=jax.ShapeDtypeStruct((QUARTER, COLS), jnp.bfloat16),
        scratch_shapes=[
            pltpu.VMEM((TRIALS, QUARTER), jnp.bfloat16),
            pltpu.VMEM((QUARTER, STEPS * TRIALS), jnp.bfloat16),
            pltpu.VMEM((TILES, QUARTER, TILE), jnp.bfloat16),
            pltpu.SemaphoreType.DMA((TILES,)),
        ],
        cost_estimate=cost(2 * STEPS * TRIALS * QUARTER * COLS, 8_000_000),
        compiler_params=params(OUTER),
        name="outer",
    )(at, *full, *pair, rates)


def whole(weights, rates):
    y, z, x, core = (lax.axis_index(a) for a in EVERY)
    at = jnp.stack([z % 4, core, y, x]).astype(jnp.int32)

    def swapped(array):
        return lax.ppermute(array, "core", SWAP)

    is_root_core = core == z // 4
    root, before, other = first(at, rates)
    theirs = swapped(give(at, lax.optimization_barrier((weights, root))[0]))
    parts = [lax.ppermute(root, EVERY, from_root(shift)) for shift in (1, 2, 3)]
    mine = keep(at, lax.optimization_barrier((weights, root))[0])
    before = jnp.where(is_root_core, before, swapped(other))
    came = jnp.where(x == y, root, parts[0] + parts[1] + parts[2])
    grad, before = lax.optimization_barrier(
        (jnp.where(is_root_core, came, swapped(came)), before)
    )
    pair = (grad,)
    full = []
    for step in range(STEPS - 1, 0, -1):
        sums, whole_grad = back(at, pair, mine, theirs)
        full.append(whole_grad)
        sums = lax.all_to_all(sums.reshape(Y * Z, SLICE, HALF), ("y", "z"), 0, 0, tiled=True)
        sums = jnp.sum(sums.astype(jnp.float32), axis=0)
        rate = before[step - 1].astype(jnp.float32)
        share = (sums * (1.0 - rate * rate)).astype(jnp.bfloat16)
        other = swapped(share)
        share = jnp.where(
            core == 0, jnp.concatenate([share, other], 1), jnp.concatenate([other, share], 1)
        )
        slices = jnp.stack([lax.ppermute(share, EVERY, across(j)) for j in range(2)])
        pair = (slices, swapped(slices))
    return outer(at, full, pair, rates)


def solution(mesh):
    fine = Mesh(mesh.devices.reshape(Y, Z, X, C), EVERY)
    in_specs = (P(("y", "z"), ("x", "core")), P(None, ("x", "core"), None))
    out_specs = P(("y", "z"), ("x", "core"))
    return jax.shard_map(whole, mesh=fine, in_specs=in_specs, out_specs=out_specs, check_vma=False)
```

```python
import jax
import jax.numpy as jnp
from jax import lax
from jax.experimental import pallas as pl
from jax.experimental.pallas import tpu as pltpu
from jax.sharding import Mesh, PartitionSpec as P

STEPS = 4
Y, Z, X, C = 4, 8, 4, 2
EVERY = ("y", "z", "x", "core")
SWAP = [(0, 1), (1, 0)]
HALF = 384
QUARTER = 768
TRIALS = 128
SLICE = 32
FIRST, BACK, OUTER, KEEP = 52, 8, 24, 48
COLS = 3072
VMEM = pl.BlockSpec(memory_space=pltpu.VMEM)
SMEM = pl.BlockSpec(memory_space=pltpu.SMEM)
HBM = pl.BlockSpec(memory_space=pltpu.HBM)


def flat(y, z, x, core):
    return ((y % Y * Z + z) * X + x % X) * C + core


def across(j):
    return [
        (flat(y, z, x, core), flat(x, z, y + 2 * j + core, core))
        for y in range(Y) for z in range(Z) for x in range(X) for core in range(C)
    ]


def from_root(shift):
    return [(flat(y, z, y, z // 4), flat(y, z, y + shift, z // 4)) for y in range(Y) for z in range(Z)]


def params(mib):
    return pltpu.CompilerParams(vmem_limit_bytes=mib << 20)


def cost(flops, moved):
    return pl.CostEstimate(flops=flops, bytes_accessed=moved, transcendentals=0)


def first_kernel(at_ref, rates_ref, out_ref, mine_ref, theirs_ref, last_ref, zero_ref, held_ref, turned_ref, sems):
    core = at_ref[1]
    rows = pl.ds(pl.multiple_of(at_ref[0] * QUARTER, 16), QUARTER)
    copies = [
        pltpu.make_async_copy(rates_ref.at[STEPS, rows], last_ref, sems.at[0]),
        pltpu.make_async_copy(rates_ref.at[0, rows], zero_ref, sems.at[1]),
        pltpu.make_async_copy(rates_ref.at[1:STEPS, rows], held_ref, sems.at[2]),
    ]
    for copy in copies:
        copy.start()
    copies[0].wait()
    copies[1].wait()
    last = last_ref[...].astype(jnp.float32)
    zero = zero_ref[...].astype(jnp.float32)
    out_ref[...] = ((last - zero) * (1.0 - last * last)).astype(jnp.bfloat16).T
    copies[2].wait()
    slot = pl.ds(pl.multiple_of(at_ref[2] * SLICE, SLICE), SLICE)
    for t in range(STEPS - 1):
        turned_ref[...] = held_ref[t].T
        for ref, part in ((theirs_ref, 1 - core), (mine_ref, core)):
            ref[t] = turned_ref[slot, pl.ds(pl.multiple_of(part * HALF, 128), HALF)]


def first(at, rates):
    small = jax.ShapeDtypeStruct((STEPS - 1, SLICE, HALF), jnp.bfloat16)
    return pl.pallas_call(
        first_kernel,
        in_specs=[SMEM, HBM],
        out_specs=[VMEM] * 3,
        out_shape=[jax.ShapeDtypeStruct((TRIALS, QUARTER), jnp.bfloat16), small, small],
        scratch_shapes=[
            pltpu.VMEM((QUARTER, TRIALS), jnp.bfloat16),
            pltpu.VMEM((QUARTER, TRIALS), jnp.bfloat16),
            pltpu.VMEM((STEPS - 1, QUARTER, TRIALS), jnp.bfloat16),
            pltpu.VMEM((TRIALS, QUARTER), jnp.bfloat16),
            pltpu.SemaphoreType.DMA((3,)),
        ],
        compiler_params=params(FIRST),
        name="first",
    )(at, rates)


def split_kernel(at_ref, w_ref, mine_ref, theirs_ref, held_ref, sems):
    core = at_ref[1]

    def columns(q, part):
        return pl.ds(pl.multiple_of((2 * q + part) * HALF, 128), HALF)

    took = [
        pltpu.make_async_copy(w_ref.at[:, columns(q, 1 - core)], held_ref.at[q], sems.at[0, q])
        for q in range(4)
    ]
    kept = [
        pltpu.make_async_copy(w_ref.at[:, columns(q, core)], mine_ref.at[q], sems.at[1, q])
        for q in range(4)
    ]
    gave = [pltpu.make_async_copy(held_ref.at[q], theirs_ref.at[q], sems.at[2, q]) for q in range(4)]
    for copy in took + kept:
        copy.start()
    for q in range(4):
        took[q].wait()
        gave[q].start()
    for copy in kept + gave:
        copy.wait()


def split(at, weights):
    shape = jax.ShapeDtypeStruct((4, QUARTER, HALF), jnp.bfloat16)
    return pl.pallas_call(
        split_kernel,
        in_specs=[SMEM, HBM],
        out_specs=[VMEM, HBM],
        out_shape=[shape, shape],
        scratch_shapes=[
            pltpu.VMEM((4, QUARTER, HALF), jnp.bfloat16),
            pltpu.SemaphoreType.DMA((3, 4)),
        ],
        cost_estimate=cost(0, 9_437_184),
        compiler_params=params(KEEP),
        name="split",
    )(at, weights)


def fill(at_ref, pair_refs, g_ref):
    core, x = at_ref[1], at_ref[3]
    if len(pair_refs) == 1:
        g_ref[...] = pair_refs[0][...]
        return
    for ref, part in zip(pair_refs, (core, 1 - core)):
        for j in range(2):
            slot = (x + 2 * X - 2 * j - part) % X
            g_ref[pl.ds(pl.multiple_of(slot * SLICE, SLICE), SLICE), :] = ref[j]


def back_kernel(at_ref, *refs):
    *pair_refs, mine_ref, theirs_ref, out_ref, g_ref, held_ref, sems = refs
    core = at_ref[1]
    copies = [
        pltpu.make_async_copy(theirs_ref.at[q], held_ref.at[q], sems.at[q]) for q in range(4)
    ]
    for copy in copies:
        copy.start()
    fill(at_ref, pair_refs, g_ref)
    for ref, block in ((mine_ref, core), (held_ref, 1 - core)):
        for q in range(4):
            if ref is held_ref:
                copies[q].wait()
            got = jnp.dot(g_ref[...], ref[q], preferred_element_type=jnp.float32)
            got = got.astype(jnp.bfloat16)
            for part in range(Y):
                out_ref[part, block * 4 + q] = got[part * SLICE : (part + 1) * SLICE]


def back(at, pair, mine, theirs):
    return pl.pallas_call(
        back_kernel,
        in_specs=[SMEM] + [VMEM] * len(pair) + [VMEM, HBM],
        out_specs=[VMEM, VMEM],
        out_shape=[
            jax.ShapeDtypeStruct((Y, 8, SLICE, HALF), jnp.bfloat16),
            jax.ShapeDtypeStruct((TRIALS, QUARTER), jnp.bfloat16),
        ],
        scratch_shapes=[
            pltpu.VMEM((4, QUARTER, HALF), jnp.bfloat16),
            pltpu.SemaphoreType.DMA((4,)),
        ],
        cost_estimate=cost(2 * TRIALS * QUARTER * COLS, 6_000_000),
        compiler_params=params(BACK),
        name="back",
    )(at, *pair, mine, theirs)


TILE = 512
TILES = COLS // TILE


def outer_kernel(
    at_ref, g4, g3, g2, first_ref, second_ref, rates_ref, out_ref, g_ref, turned_ref, done_ref, sems
):
    went = [
        pltpu.make_async_copy(done_ref.at[j], out_ref.at[:, pl.ds(j * TILE, TILE)], sems.at[j])
        for j in range(TILES)
    ]
    for t, ref in ((3, g4), (2, g3), (1, g2)):
        turned_ref[:, t * TRIALS : (t + 1) * TRIALS] = ref[...].T
    fill(at_ref, (first_ref, second_ref), g_ref)
    turned_ref[:, :TRIALS] = g_ref[...].T
    for j in range(TILES):
        part = slice(j * TILE, (j + 1) * TILE)
        before = jnp.concatenate([rates_ref[t, part, :] for t in range(STEPS)], axis=1)
        done_ref[j] = lax.dot_general(
            turned_ref[...], before, (((1,), (1,)), ((), ())), preferred_element_type=jnp.float32
        ).astype(jnp.bfloat16)
        went[j].start()
    for copy in went:
        copy.wait()


def outer(at, full, pair, rates):
    return pl.pallas_call(
        outer_kernel,
        in_specs=[SMEM] + [VMEM] * 6,
        out_specs=HBM,
        out_shape=jax.ShapeDtypeStruct((QUARTER, COLS), jnp.bfloat16),
        scratch_shapes=[
            pltpu.VMEM((TRIALS, QUARTER), jnp.bfloat16),
            pltpu.VMEM((QUARTER, STEPS * TRIALS), jnp.bfloat16),
            pltpu.VMEM((TILES, QUARTER, TILE), jnp.bfloat16),
            pltpu.SemaphoreType.DMA((TILES,)),
        ],
        cost_estimate=cost(2 * STEPS * TRIALS * QUARTER * COLS, 8_000_000),
        compiler_params=params(OUTER),
        name="outer",
    )(at, *full, *pair, rates)


def whole(weights, rates):
    y, z, x, core = (lax.axis_index(a) for a in EVERY)
    at = jnp.stack([z % 4, core, y, x]).astype(jnp.int32)

    def swapped(array):
        return lax.ppermute(array, "core", SWAP)

    is_root_core = core == z // 4
    root, before, other = first(at, rates)
    far = lax.ppermute(root, EVERY, from_root(2))
    parts = [far] + [lax.ppermute(root, EVERY, from_root(shift)) for shift in (1, 3)]
    mine, theirs = split(at, lax.optimization_barrier((weights, root))[0])
    theirs = swapped(theirs)
    before = jnp.where(is_root_core, before, swapped(other))
    came = jnp.where(x == y, root, parts[0] + parts[1] + parts[2])
    grad, before = lax.optimization_barrier(
        (jnp.where(is_root_core, came, swapped(came)), before)
    )
    pair = (grad,)
    full = []
    for step in range(STEPS - 1, 0, -1):
        sums, whole_grad = back(at, pair, mine, theirs)
        full.append(whole_grad)
        sums = lax.all_to_all(sums.reshape(Y * Z, SLICE, HALF), ("y", "z"), 0, 0, tiled=True)
        sums = jnp.sum(sums.astype(jnp.float32), axis=0)
        rate = before[step - 1].astype(jnp.float32)
        share = (sums * (1.0 - rate * rate)).astype(jnp.bfloat16)
        other = swapped(share)
        share = jnp.where(
            core == 0, jnp.concatenate([share, other], 1), jnp.concatenate([other, share], 1)
        )
        slices = jnp.stack([lax.ppermute(share, EVERY, across(j)) for j in range(2)])
        pair = (slices, swapped(slices))
    return outer(at, full, pair, rates)


def solution(mesh):
    fine = Mesh(mesh.devices.reshape(Y, Z, X, C), EVERY)
    in_specs = (P(("y", "z"), ("x", "core")), P(None, ("x", "core"), None))
    out_specs = P(("y", "z"), ("x", "core"))
    return jax.shard_map(whole, mesh=fine, in_specs=in_specs, out_specs=out_specs, check_vma=False)
```

```python
import jax
import jax.numpy as jnp
from jax import lax
from jax.experimental import pallas as pl
from jax.experimental.pallas import tpu as pltpu
from jax.sharding import Mesh, PartitionSpec as P

STEPS = 4
Y, Z, X, C = 4, 8, 4, 2
EVERY = ("y", "z", "x", "core")
SWAP = [(0, 1), (1, 0)]
HALF = 384
QUARTER = 768
TRIALS = 128
SLICE = 32
FIRST, BACK, OUTER, KEEP = 52, 48, 24, 48
COLS = 3072
VMEM = pl.BlockSpec(memory_space=pltpu.VMEM)
SMEM = pl.BlockSpec(memory_space=pltpu.SMEM)
HBM = pl.BlockSpec(memory_space=pltpu.HBM)


def flat(y, z, x, core):
    return ((y % Y * Z + z) * X + x % X) * C + core


def across(j):
    return [
        (flat(y, z, x, core), flat(x, z, y + 2 * j + core, core))
        for y in range(Y) for z in range(Z) for x in range(X) for core in range(C)
    ]


def from_root(shift):
    return [(flat(y, z, y, z // 4), flat(y, z, y + shift, z // 4)) for y in range(Y) for z in range(Z)]


def params(mib):
    return pltpu.CompilerParams(vmem_limit_bytes=mib << 20)


def cost(flops, moved):
    return pl.CostEstimate(flops=flops, bytes_accessed=moved, transcendentals=0)


def first_kernel(at_ref, rates_ref, out_ref, mine_ref, theirs_ref, last_ref, zero_ref, held_ref, turned_ref, sems):
    core = at_ref[1]
    rows = pl.ds(pl.multiple_of(at_ref[0] * QUARTER, 16), QUARTER)
    copies = [
        pltpu.make_async_copy(rates_ref.at[STEPS, rows], last_ref, sems.at[0]),
        pltpu.make_async_copy(rates_ref.at[0, rows], zero_ref, sems.at[1]),
        pltpu.make_async_copy(rates_ref.at[1:STEPS, rows], held_ref, sems.at[2]),
    ]
    for copy in copies:
        copy.start()
    copies[0].wait()
    copies[1].wait()
    last = last_ref[...].astype(jnp.float32)
    zero = zero_ref[...].astype(jnp.float32)
    out_ref[...] = ((last - zero) * (1.0 - last * last)).astype(jnp.bfloat16).T
    copies[2].wait()
    slot = pl.ds(pl.multiple_of(at_ref[2] * SLICE, SLICE), SLICE)
    for t in range(STEPS - 1):
        turned_ref[...] = held_ref[t].T
        for ref, part in ((theirs_ref, 1 - core), (mine_ref, core)):
            ref[t] = turned_ref[slot, pl.ds(pl.multiple_of(part * HALF, 128), HALF)]


def first(at, rates):
    small = jax.ShapeDtypeStruct((STEPS - 1, SLICE, HALF), jnp.bfloat16)
    return pl.pallas_call(
        first_kernel,
        in_specs=[SMEM, HBM],
        out_specs=[VMEM] * 3,
        out_shape=[jax.ShapeDtypeStruct((TRIALS, QUARTER), jnp.bfloat16), small, small],
        scratch_shapes=[
            pltpu.VMEM((QUARTER, TRIALS), jnp.bfloat16),
            pltpu.VMEM((QUARTER, TRIALS), jnp.bfloat16),
            pltpu.VMEM((STEPS - 1, QUARTER, TRIALS), jnp.bfloat16),
            pltpu.VMEM((TRIALS, QUARTER), jnp.bfloat16),
            pltpu.SemaphoreType.DMA((3,)),
        ],
        compiler_params=params(FIRST),
        name="first",
    )(at, rates)


def columns(q, part):
    return pl.ds(pl.multiple_of((2 * q + part) * HALF, 128), HALF)


def keep_kernel(at_ref, w_ref, mine_ref, sems):
    copies = [
        pltpu.make_async_copy(w_ref.at[:, columns(q, at_ref[1])], mine_ref.at[q], sems.at[q])
        for q in range(4)
    ]
    for copy in copies:
        copy.start()
    for copy in copies:
        copy.wait()


def keep(at, weights):
    return pl.pallas_call(
        keep_kernel,
        in_specs=[SMEM, HBM],
        out_specs=VMEM,
        out_shape=jax.ShapeDtypeStruct((4, QUARTER, HALF), jnp.bfloat16),
        scratch_shapes=[pltpu.SemaphoreType.DMA((4,))],
        cost_estimate=cost(0, 4_718_592),
        compiler_params=params(KEEP),
        name="keep",
    )(at, weights)


def fill(at_ref, pair_refs, g_ref):
    core, x = at_ref[1], at_ref[3]
    if len(pair_refs) == 1:
        g_ref[...] = pair_refs[0][...]
        return
    for ref, part in zip(pair_refs, (core, 1 - core)):
        for j in range(2):
            slot = (x + 2 * X - 2 * j - part) % X
            g_ref[pl.ds(pl.multiple_of(slot * SLICE, SLICE), SLICE), :] = ref[j]


def back_kernel(at_ref, *refs):
    *pair_refs, mine_ref, theirs_ref, out_ref, g_ref, held_ref, sems = refs
    core = at_ref[1]
    copies = [
        pltpu.make_async_copy(theirs_ref.at[:, columns(q, core)], held_ref.at[q], sems.at[q])
        for q in range(4)
    ]
    for copy in copies:
        copy.start()
    fill(at_ref, pair_refs, g_ref)
    for ref, block in ((mine_ref, core), (held_ref, 1 - core)):
        for q in range(4):
            if ref is held_ref:
                copies[q].wait()
            got = jnp.dot(g_ref[...], ref[q], preferred_element_type=jnp.float32)
            got = got.astype(jnp.bfloat16)
            for part in range(Y):
                out_ref[part, block * 4 + q] = got[part * SLICE : (part + 1) * SLICE]


def back(at, pair, mine, theirs):
    return pl.pallas_call(
        back_kernel,
        in_specs=[SMEM] + [VMEM] * len(pair) + [VMEM, HBM],
        out_specs=[VMEM, VMEM],
        out_shape=[
            jax.ShapeDtypeStruct((Y, 8, SLICE, HALF), jnp.bfloat16),
            jax.ShapeDtypeStruct((TRIALS, QUARTER), jnp.bfloat16),
        ],
        scratch_shapes=[
            pltpu.VMEM((4, QUARTER, HALF), jnp.bfloat16),
            pltpu.SemaphoreType.DMA((4,)),
        ],
        cost_estimate=cost(2 * TRIALS * QUARTER * COLS, 6_000_000),
        compiler_params=params(BACK),
        name="back",
    )(at, *pair, mine, theirs)


TILE = 512
TILES = COLS // TILE


def outer_kernel(
    at_ref, g4, g3, g2, first_ref, second_ref, rates_ref, out_ref, g_ref, turned_ref, done_ref, sems
):
    went = [
        pltpu.make_async_copy(done_ref.at[j], out_ref.at[:, pl.ds(j * TILE, TILE)], sems.at[j])
        for j in range(TILES)
    ]
    for t, ref in ((3, g4), (2, g3), (1, g2)):
        turned_ref[:, t * TRIALS : (t + 1) * TRIALS] = ref[...].T
    fill(at_ref, (first_ref, second_ref), g_ref)
    turned_ref[:, :TRIALS] = g_ref[...].T
    for j in range(TILES):
        part = slice(j * TILE, (j + 1) * TILE)
        before = jnp.concatenate([rates_ref[t, part, :] for t in range(STEPS)], axis=1)
        done_ref[j] = lax.dot_general(
            turned_ref[...], before, (((1,), (1,)), ((), ())), preferred_element_type=jnp.float32
        ).astype(jnp.bfloat16)
        went[j].start()
    for copy in went:
        copy.wait()


def outer(at, full, pair, rates):
    return pl.pallas_call(
        outer_kernel,
        in_specs=[SMEM] + [VMEM] * 6,
        out_specs=HBM,
        out_shape=jax.ShapeDtypeStruct((QUARTER, COLS), jnp.bfloat16),
        scratch_shapes=[
            pltpu.VMEM((TRIALS, QUARTER), jnp.bfloat16),
            pltpu.VMEM((QUARTER, STEPS * TRIALS), jnp.bfloat16),
            pltpu.VMEM((TILES, QUARTER, TILE), jnp.bfloat16),
            pltpu.SemaphoreType.DMA((TILES,)),
        ],
        cost_estimate=cost(2 * STEPS * TRIALS * QUARTER * COLS, 8_000_000),
        compiler_params=params(OUTER),
        name="outer",
    )(at, *full, *pair, rates)


def whole(weights, rates):
    y, z, x, core = (lax.axis_index(a) for a in EVERY)
    at = jnp.stack([z % 4, core, y, x]).astype(jnp.int32)

    def swapped(array):
        return lax.ppermute(array, "core", SWAP)

    is_root_core = core == z // 4
    root, before, other = first(at, rates)
    theirs = swapped(lax.optimization_barrier((weights, root))[0])
    parts = [lax.ppermute(root, EVERY, from_root(shift)) for shift in (1, 2, 3)]
    mine = keep(at, lax.optimization_barrier((weights, root))[0])
    before = jnp.where(is_root_core, before, swapped(other))
    came = jnp.where(x == y, root, parts[0] + parts[1] + parts[2])
    grad, before = lax.optimization_barrier(
        (jnp.where(is_root_core, came, swapped(came)), before)
    )
    pair = (grad,)
    full = []
    for step in range(STEPS - 1, 0, -1):
        sums, whole_grad = back(at, pair, mine, theirs)
        full.append(whole_grad)
        sums = lax.all_to_all(sums.reshape(Y * Z, SLICE, HALF), ("y", "z"), 0, 0, tiled=True)
        sums = jnp.sum(sums.astype(jnp.float32), axis=0)
        rate = before[step - 1].astype(jnp.float32)
        share = (sums * (1.0 - rate * rate)).astype(jnp.bfloat16)
        other = swapped(share)
        share = jnp.where(
            core == 0, jnp.concatenate([share, other], 1), jnp.concatenate([other, share], 1)
        )
        slices = jnp.stack([lax.ppermute(share, EVERY, across(j)) for j in range(2)])
        pair = (slices, swapped(slices))
    return outer(at, full, pair, rates)


def solution(mesh):
    fine = Mesh(mesh.devices.reshape(Y, Z, X, C), EVERY)
    in_specs = (P(("y", "z"), ("x", "core")), P(None, ("x", "core"), None))
    out_specs = P(("y", "z"), ("x", "core"))
    return jax.shard_map(whole, mesh=fine, in_specs=in_specs, out_specs=out_specs, check_vma=False)
```
